512 devices in a mesh: grp: 16 (over z_lo, y), dev: 32 (over x, z_hi, core).
Axes of the slice: x: 4, y: 4, z: 16 (z_hi: 4, z_lo: 4; z = z_hi * 4 + z_lo), core: 2. Of those that a mesh axis runs over, the one named last changes fastest.
Arguments:
- embedding: bfloat16 [524288, 256], P(('grp', 'dev')), may hold values from -6 to 6
- cotangent: bfloat16 [524288, 256], P(('grp', 'dev')), may hold values from -6 to 6
- fractional: bfloat16 [3, 524288], P(None, ('grp', 'dev')), may hold values from 0 to 1
- wave_index: int32 [3, 512], replicated, may hold values from -8 to 8
- tile_pairs: int32 [12288, 2], P(('grp', 'dev')), may hold values from 0 to 15, as said below
- counts: int32 [512], P(('grp', 'dev')), may hold values from 3 to 24, as said below
- wave_filter: float32 [512, 256], replicated, may hold values from -0.25 to 0.25
- short_weight: bfloat16 [256, 256], replicated, may hold values from -0.375 to 0.375
Outputs:
- message: bfloat16 [524288, 256], P(('grp', 'dev'))
- embedding_grad: bfloat16 [524288, 256], P(('grp', 'dev'))
The draws below stay inside these ranges and needn't reach their ends.
Inputs may be any that keep to these rules, and one draw needn't show every extreme that they name: `tile_pairs`: in each block's 24 rows, column 0 is one of the block's 8 tiles and column 1 one of 16 tiles: the block's own, then the next block's. The first row of every block names a tile of the next block. `counts`: some block has exactly 24 live rows in every draw.
All inputs are finite; a program needn't handle non-finite values.
Results may differ from the reference program's by a relative error of at most 0.0059.
Values may be sent and summed in bfloat16 or wider, within the bound.
No kernel may reach another device: no remote copies, remote signals or barrier semaphores. Data moves between devices by JAX's collectives and lax.ppermute only.
A program may use at most 64 MiB of HBM per device.

```python
import math
import jax
import jax.numpy as jnp
from jax import lax

C = 256
K = 512
TILE = 128
ATOM_DEV = 1024
PAIRS_MAX = 24
BLOCKS = 512
ATOMS = 524288


def draw_tile_pairs(key, part):
    tiles = ATOM_DEV // TILE
    firsts = jax.random.randint(jax.random.fold_in(key, 21), (BLOCKS * PAIRS_MAX,), 0, tiles)
    seconds = jax.random.randint(jax.random.fold_in(key, 22), (BLOCKS * PAIRS_MAX,), 0, 2 * tiles)
    reaching = tiles + jax.random.randint(jax.random.fold_in(key, 23), (BLOCKS * PAIRS_MAX,), 0, tiles)
    rows = jnp.arange(BLOCKS * PAIRS_MAX, dtype=jnp.int32)
    seconds = jnp.where(rows % PAIRS_MAX == 0, reaching, seconds)
    seconds = jnp.where(rows == 0, 2 * tiles - 1, seconds)
    seconds = jnp.where(rows == 1, 0, seconds)
    firsts = jnp.where(rows == 1, 0, firsts)
    return jnp.stack([firsts, seconds], axis=1).astype(jnp.int32)


def draw_counts(key, part):
    levels = jax.random.randint(jax.random.fold_in(key, 31), (BLOCKS,), 0, 4)
    powers = jnp.left_shift(jnp.ones((BLOCKS,), jnp.int32), levels.astype(jnp.int32))
    shares = (PAIRS_MAX + powers - 1) // powers
    busiest = jax.random.randint(jax.random.fold_in(key, 32), (), 0, BLOCKS)
    return jnp.where(jnp.arange(BLOCKS) == busiest, PAIRS_MAX, shares).astype(jnp.int32)


def with_ends(result, rng, low, high):
    longest = result.shape.index(max(result.shape))
    spots = []
    for shift in (0, 1):
        where = [jax.random.randint(jax.random.fold_in(rng, axis), (), 0, length) for axis, length in enumerate(result.shape)]
        where[longest] = (where[longest] + shift) % result.shape[longest]
        spots.append(tuple(where))
    return result.at[spots[0]].set(low).at[spots[1]].set(high)


def steps_of(stream_key, shape, cuts, smallest, largest):
    loudness, own = 1.0, jax.random.fold_in(stream_key, 6)
    for dim, parts in cuts:
        draws = jnp.exp(jax.random.uniform(jax.random.fold_in(own, dim), (parts,), jnp.float32, smallest / len(cuts), largest / len(cuts)))
        loudness = loudness * jnp.repeat(draws, shape[dim] // parts).reshape([-1 if axis == dim else 1 for axis in range(len(shape))])
    return loudness


def noise(own_key, shape, deviation, reach, shards=(), kind=jnp.bfloat16):
    array = deviation * jax.random.normal(own_key, shape, jnp.float32)
    if shards:
        array = array * steps_of(own_key, shape, shards, -0.22, 0.18)
    return jnp.clip(array, -reach, reach).astype(kind)


def setup_inputs(seed: int = 0) -> dict:
    streams_of = jax.random.split(jax.random.key(seed), 9)
    return {
        "embedding": noise(streams_of[0], (ATOMS, C), 1.0, 6.0, ((0, 512),)),
        "cotangent": noise(streams_of[1], (ATOMS, C), 1.0, 6.0, ((0, 512),)),
        "fractional": jnp.clip(1.0 * jax.random.uniform(streams_of[2], (3, ATOMS), jnp.float32) ** steps_of(streams_of[2], (3, ATOMS), ((1, 512),), -0.2, 0.2), 0.0, 1.0).astype(jnp.bfloat16),
        "wave_index": with_ends(jax.random.randint(streams_of[3], (3, K), -8, 9), jax.random.fold_in(streams_of[3], 1), -8, 8).astype(jnp.int32),
        "tile_pairs": draw_tile_pairs(jax.random.fold_in(streams_of[8], 71), 0),
        "counts": draw_counts(jax.random.fold_in(streams_of[8], 71), 0),
        "wave_filter": noise(streams_of[6], (K, C), K ** -0.5, 0.25, (), jnp.float32),
        "short_weight": noise(streams_of[7], (C, C), C ** -0.5, 0.375),
    }


two_pi = 2.0 * math.pi

def trig_table(places, wave_index):
    phase = two_pi * jnp.dot(places.astype(jnp.float32).T, wave_index.astype(jnp.float32), precision=lax.Precision.HIGHEST)
    return jnp.concatenate([jnp.cos(phase), jnp.sin(phase)], axis=1).astype(jnp.bfloat16)

def pair_kernel(left_places, right_places):
    left = left_places.astype(jnp.float32)
    right = right_places.astype(jnp.float32)
    wave = jnp.sin(math.pi * (left[:, :, None] - right[:, None, :]))
    spread = jnp.exp(-2.0 * lax.optimization_barrier(jnp.sum(wave * wave, axis=0)))
    return (spread / math.sqrt(left.shape[1])).astype(jnp.bfloat16)

def reference(embedding, cotangent, fractional, wave_index, tile_pairs, counts, wave_filter, short_weight):
    channels = embedding.shape[1]
    tile_count = ATOM_DEV // TILE
    inv_root = 1.0 / math.sqrt(ATOMS)
    place_blocks = fractional.reshape(3, BLOCKS, ATOM_DEV).transpose(1, 0, 2)
    embed_blocks = embedding.reshape(BLOCKS, ATOM_DEV, channels)
    cot_blocks = cotangent.reshape(BLOCKS, ATOM_DEV, channels)

    def add_block(total, items):
        places, embed_rows, cot_rows = items
        table = trig_table(places, wave_index)
        dims = (((0,), (0,)), ((), ()))
        first_half = lax.dot_general(table, embed_rows, dims, preferred_element_type=jnp.float32)
        second_half = lax.dot_general(table, cot_rows, dims, preferred_element_type=jnp.float32)
        return (total + jnp.concatenate([first_half, second_half], axis=1), None)
    summed, _unused = lax.scan(add_block, jnp.zeros((2 * K, 2 * channels), jnp.float32), (place_blocks, embed_blocks, cot_blocks))
    doubled = jnp.concatenate([wave_filter, wave_filter], axis=0)
    tiled = jnp.concatenate([doubled, doubled], axis=1)
    coeffs = (summed * tiled * inv_root).astype(jnp.bfloat16)
    projected = jnp.dot(embedding, short_weight, preferred_element_type=jnp.float32).astype(jnp.bfloat16)
    proj_tiles = projected.reshape(BLOCKS, tile_count, TILE, channels)
    place_tiles = fractional.reshape(3, BLOCKS, tile_count, TILE).transpose(1, 2, 0, 3)
    cot_tiles = cotangent.reshape(BLOCKS, tile_count, TILE, channels)
    pair_blocks = tile_pairs.reshape(BLOCKS, PAIRS_MAX, 2)

    def near_block(index):
        after = (index + 1) % BLOCKS
        places = jnp.concatenate([place_tiles[index], place_tiles[after]], axis=0)
        sources = jnp.concatenate([proj_tiles[index], proj_tiles[after]], axis=0)
        targets = cot_tiles[index]
        pairs = pair_blocks[index]
        firsts = pairs[:, 0].astype(jnp.int32)
        seconds = pairs[:, 1].astype(jnp.int32)
        kernels = jax.vmap(pair_kernel)(places[firsts], places[seconds]).astype(jnp.float32)
        live = (jnp.arange(PAIRS_MAX, dtype=jnp.int32) < counts[index])[:, None, None]
        ahead = jnp.einsum('pij,pjc->pic', kernels, sources[seconds].astype(jnp.float32))
        behind = jnp.einsum('pij,pic->pjc', kernels, targets[firsts].astype(jnp.float32))
        forward = jax.ops.segment_sum(jnp.where(live, ahead, 0.0), firsts, num_segments=tile_count)
        backward = jax.ops.segment_sum(jnp.where(live, behind, 0.0), seconds, num_segments=2 * tile_count)
        return (forward, backward)
    start_carry = near_block(jnp.int32(BLOCKS - 1))[1][tile_count:]

    def block_outputs(carry, index):
        forward, backward = near_block(index)
        table = trig_table(place_blocks[index], wave_index)
        long_range = jnp.dot(table, coeffs, preferred_element_type=jnp.float32)
        message = (long_range[:, :channels] + forward.reshape(ATOM_DEV, channels)).astype(jnp.bfloat16)
        near_grad = (backward[:tile_count] + carry).reshape(ATOM_DEV, channels).astype(jnp.bfloat16)
        mixed = lax.dot_general(near_grad, short_weight, (((1,), (1,)), ((), ())), preferred_element_type=jnp.float32)
        gradient = (long_range[:, channels:] + mixed).astype(jnp.bfloat16)
        return (backward[tile_count:], (message, gradient))
    _unused, outputs = lax.scan(block_outputs, start_carry, jnp.arange(BLOCKS, dtype=jnp.int32))
    message, gradient = outputs
    return (message.reshape(ATOMS, channels), gradient.reshape(ATOMS, channels))
```

```python
import functools
import math

import jax
import jax.numpy as jnp
from jax import lax
from jax.experimental import pallas as pl
from jax.experimental.pallas import tpu as pltpu
from jax.sharding import Mesh
from jax.sharding import PartitionSpec as P


TILE = 128
FINE = ("z_lo", "y", "x", "z_hi", "core")
ALONG_Z = ("z_lo", "z_hi")
F32, BF16 = jnp.float32, jnp.bfloat16
VMEM = pl.BlockSpec(memory_space=pltpu.VMEM)
SMEM = pl.BlockSpec(memory_space=pltpu.SMEM)

COS = (
    0.9999999889445764,
    -19.73920446657614,
    64.93911592834654,
    -85.45011342750612,
    60.167429791960785,
    -25.966884612677454,
    6.527705963152031,
)
SIN = (
    6.283185302468581,
    -41.34170039298386,
    81.60513081114435,
    -76.70300555818746,
    42.02585148963868,
    -14.899578436725896,
    3.2377800860428168,
)


def cos_sin(turns):
    r = turns - jnp.floor(turns + 0.5)
    u = r * r
    c, s = COS[-1], SIN[-1]
    for k in COS[-2::-1]:
        c = c * u + k
    for k in SIN[-2::-1]:
        s = s * u + k
    return c, s * r


def dot(a, b, dims=((1,), (0,))):
    return lax.dot_general(a, b, (dims, ((), ())), preferred_element_type=F32)


def padded(rows):
    rows = rows.astype(F32)
    return jnp.concatenate([rows, jnp.zeros((5, rows.shape[1]), F32)], axis=0)


def sums_kernel(seat, waves_far, places_far, left_far, right_far, out, waves, places, left, right, turns, table, sems):
    half, atoms = turns.shape
    mine = pl.ds(pl.multiple_of(seat[0] * half, half), half)
    loads = [
        pltpu.make_async_copy(waves_far.at[:, mine], waves, sems.at[0]),
        pltpu.make_async_copy(places_far, places, sems.at[1]),
        pltpu.make_async_copy(left_far, left, sems.at[2]),
        pltpu.make_async_copy(right_far, right, sems.at[3]),
    ]
    for load in loads:
        load.start()
    loads[0].wait()
    loads[1].wait()
    turns[...] = dot(padded(waves[...]).astype(BF16), padded(places[...]).astype(BF16), ((0,), (0,)))

    @pl.loop(0, half // 16)
    def _(i):
        top = pl.ds(pl.multiple_of(i * 16, 16), 16)
        low = pl.ds(pl.multiple_of(half + i * 16, 16), 16)
        for j in range(atoms // 256):
            cols = pl.ds(j * 256, 256)
            c, s = cos_sin(turns[top, cols])
            table[top, cols] = c.astype(BF16)
            table[low, cols] = s.astype(BF16)

    for side, ref in enumerate((left, right)):
        loads[2 + side].wait()
        for block in range(2):
            part = dot(table[block * half : block * half + half, :], ref[...])
            for r in range(half // 8):
                i, k = divmod(block * (half // 8) + r, 4)
                for q in range(2):
                    out[i, k * 4 + side * 2 + q] = part[8 * r : 8 * r + 8, 128 * q : 128 * q + 128]


def partial_sums(seat, waves, places, left, right):
    half, atoms = waves.shape[1] // 2, places.shape[1]
    return pl.pallas_call(
        sums_kernel,
        out_shape=jax.ShapeDtypeStruct((16, 16, 8, 128), F32),
        in_specs=[SMEM] + [pl.BlockSpec(memory_space=pltpu.HBM)] * 4,
        out_specs=VMEM,
        scratch_shapes=[
            pltpu.VMEM((3, half), waves.dtype),
            pltpu.VMEM(places.shape, BF16),
            pltpu.VMEM(left.shape, BF16),
            pltpu.VMEM(right.shape, BF16),
            pltpu.VMEM((half, atoms), F32),
            pltpu.VMEM((2 * half, atoms), BF16),
            pltpu.SemaphoreType.DMA((4,)),
        ],
        compiler_params=pltpu.CompilerParams(vmem_limit_bytes=12 << 20),
        cost_estimate=pl.CostEstimate(
            flops=4 * half * atoms * 512, bytes_accessed=2 << 20, transcendentals=0
        ),
        name="sums",
    )(seat, *(pltpu.with_memory_space_constraint(v, pltpu.HBM) for v in (waves, places, left, right)))


def add_kernel(a, b, out):
    @pl.loop(0, a.shape[0])
    def _(i):
        out[i] = a[i] + b[i]


def add(a, b):
    return pl.pallas_call(
        add_kernel,
        out_shape=jax.ShapeDtypeStruct(a.shape, F32),
        in_specs=[VMEM] * 2,
        out_specs=VMEM,
        compiler_params=pltpu.CompilerParams(vmem_limit_bytes=4 << 20),
        name="add",
    )(a, b)


def gather_sum_kernel(a, out):
    @pl.loop(0, out.shape[0])
    def _(i):
        total = a[0, i]
        for k in range(1, a.shape[0]):
            total = total + a[k, i]
        out[i] = total


def gather_sum(a):
    return pl.pallas_call(
        gather_sum_kernel,
        out_shape=jax.ShapeDtypeStruct(a.shape[1:], F32),
        in_specs=[VMEM],
        out_specs=VMEM,
        compiler_params=pltpu.CompilerParams(vmem_limit_bytes=4 << 20),
        name="plane_sum",
    )(a)


def coefficients_kernel(a, scale, out):
    total = a[0]
    for k in range(1, a.shape[0]):
        total = total + a[k]
    mine = (total * scale[...]).astype(BF16)

    @pl.loop(0, out.shape[0] // 8)
    def _(i):
        for k in range(8):
            out[i * 8 + k] = mine


def coefficients(a, scale):
    return pl.pallas_call(
        coefficients_kernel,
        out_shape=jax.ShapeDtypeStruct((256, 8, 128), BF16),
        in_specs=[VMEM] * 2,
        out_specs=VMEM,
        compiler_params=pltpu.CompilerParams(vmem_limit_bytes=4 << 20),
        name="coefficients",
    )(a, scale)


def table_kernel(seat, waves, places, wave_filter, table, scale, turns, *, atoms_all):
    atoms, count = turns.shape
    half = count // 2
    turns[...] = dot(padded(places[...]).astype(BF16), padded(waves[...]).astype(BF16), ((0,), (0,)))

    @pl.loop(0, atoms // 16)
    def _(i):
        rows = pl.ds(pl.multiple_of(i * 16, 16), 16)
        for j in range(2):
            c, s = cos_sin(turns[rows, j * half : j * half + half])
            table[rows, 2 * j * half : (2 * j + 1) * half] = c.astype(BF16)
            table[rows, (2 * j + 1) * half : (2 * j + 2) * half] = s.astype(BF16)

    row, col = seat[1], seat[2]
    tile = wave_filter[pl.ds(pl.multiple_of(row * 8, 8), 8), pl.ds(pl.multiple_of(col * 128, 128), 128)]
    scale[...] = tile * (1.0 / math.sqrt(atoms_all))


def tables(seat, waves, places, wave_filter, atoms_all):
    atoms, count = places.shape[1], waves.shape[1]
    return pl.pallas_call(
        functools.partial(table_kernel, atoms_all=atoms_all),
        out_shape=(
            jax.ShapeDtypeStruct((atoms, 2 * count), BF16),
            jax.ShapeDtypeStruct((8, 128), F32),
        ),
        in_specs=[SMEM] + [VMEM] * 3,
        out_specs=(VMEM, VMEM),
        scratch_shapes=[pltpu.VMEM((atoms, count), F32)],
        compiler_params=pltpu.CompilerParams(vmem_limit_bytes=12 << 20),
        cost_estimate=pl.CostEstimate(flops=6 << 30, bytes_accessed=2 << 20, transcendentals=0),
        name="table",
    )(seat, waves, places, wave_filter)


def thirds(value):
    a = value.astype(BF16).astype(F32)
    b = (value - a).astype(BF16).astype(F32)
    return a, b, value - a - b


def features(places):
    coords = padded(places)
    live = lax.broadcasted_iota(jnp.int32, coords.shape, 0) < 3
    parts = [thirds(jnp.where(live, v, 0.0)) for v in cos_sin(coords)]
    left = jnp.concatenate([p[k] for k in (0, 0, 1, 1, 0, 2) for p in parts], axis=0)
    right = jnp.concatenate([p[k] for k in (0, 1, 0, 1, 2, 0) for p in parts], axis=0)
    return left, right


GROUP = 4


def near_kernel(
    pairs, count, embedding, embedding_above, cotangent, places, places_above, weight,
    ahead, behind, behind_next,
    projected, back, lefts, rights,
):
    atoms = embedding.shape[0]
    tiles = atoms // TILE
    projected[pl.ds(0, atoms), :] = dot(embedding[...], weight[...]).astype(BF16)
    projected[pl.ds(atoms, atoms), :] = dot(embedding_above[...], weight[...]).astype(BF16)
    left, right = features(places[...])
    _, right_above = features(places_above[...])
    lefts[...] = left.T.astype(BF16)
    for t in range(tiles):
        cut = slice(t * TILE, t * TILE + TILE)
        rights[t] = right[:, cut].astype(BF16)
        rights[tiles + t] = right_above[:, cut].astype(BF16)
    ahead[...] = jnp.zeros_like(ahead)
    back[...] = jnp.zeros_like(back)
    shift = -3.0 - 0.5 * math.log(TILE)

    def rows(t):
        return pl.ds(pl.multiple_of(t * TILE, TILE), TILE)

    @pl.loop(0, pairs.shape[0] // (2 * GROUP))
    def _(g):
        first, second, fore, rear = [], [], [], []
        for j in range(GROUP):
            p = g * GROUP + j
            u, v = pairs[2 * p], pairs[2 * p + 1]
            k = jnp.exp(dot(lefts[rows(u), :], rights[v]) + shift)
            k = jnp.where(p < count[0], k, 0.0)
            first.append(u)
            second.append(v)
            fore.append(dot(k.astype(BF16), projected[rows(v), :]))
            rear.append(dot(k.T.astype(BF16), cotangent[rows(u), :]))
        for u, v, f, r in zip(first, second, fore, rear, strict=True):
            ahead[rows(u), :] += f
            back[rows(v), :] += r

    behind[...] = back[pl.ds(0, atoms), :]
    behind_next[...] = back[pl.ds(atoms, atoms), :].astype(BF16)


def near(pairs, count, embedding, embedding_above, cotangent, places, places_above, weight):
    atoms, channels = embedding.shape
    tiles = atoms // TILE
    return pl.pallas_call(
        near_kernel,
        out_shape=(
            jax.ShapeDtypeStruct((atoms, channels), F32),
            jax.ShapeDtypeStruct((atoms, channels), F32),
            jax.ShapeDtypeStruct((atoms, channels), BF16),
        ),
        in_specs=[SMEM] * 2 + [VMEM] * 6,
        out_specs=(VMEM, VMEM, VMEM),
        scratch_shapes=[
            pltpu.VMEM((2 * atoms, channels), BF16),
            pltpu.VMEM((2 * atoms, channels), F32),
            pltpu.VMEM((atoms, 96), BF16),
            pltpu.VMEM((2 * tiles, 96, TILE), BF16),
        ],
        compiler_params=pltpu.CompilerParams(vmem_limit_bytes=16 << 20),
        cost_estimate=pl.CostEstimate(flops=10 << 30, bytes_accessed=4 << 20, transcendentals=0),
        name="near",
    )(pairs, count, embedding, embedding_above, cotangent, places, places_above, weight)


def mixed_kernel(own, below, weight, out):
    grad = (own[...] + below[...].astype(F32)).astype(BF16)
    out[...] = dot(grad, weight[...], ((1,), (1,)))


def mixing(own, below, weight):
    return pl.pallas_call(
        mixed_kernel,
        out_shape=jax.ShapeDtypeStruct(own.shape, F32),
        in_specs=[VMEM] * 3,
        out_specs=VMEM,
        compiler_params=pltpu.CompilerParams(vmem_limit_bytes=8 << 20),
        cost_estimate=pl.CostEstimate(flops=1 << 28, bytes_accessed=2 << 20, transcendentals=0),
        name="mixed",
    )(own, below, weight)


def final_kernel(order, seat, own, other, table, ahead, mixed, message, grad, matrix):
    channels = message.shape[1]

    @pl.when(pl.program_id(0) == 0)
    def _():
        for half, ref in ((seat[0], own), (1 - seat[0], other)):
            for r in range(0, 64, 2):
                rows = pl.ds(pl.multiple_of(half * 512 + 8 * r, 16), 16)
                for q in range(4):
                    pair = [ref[order[(r + d) * 4 + q]].astype(F32) for d in range(2)]
                    matrix[rows, 128 * q : 128 * q + 128] = jnp.concatenate(pair, axis=0).astype(BF16)

    message[...] = (dot(table[...], matrix[:, :channels]) + ahead[...]).astype(BF16)
    grad[...] = (dot(table[...], matrix[:, channels:]) + mixed[...]).astype(BF16)


def final(order, seat, own, other, table, ahead, mixed, steps=4):
    atoms, channels = ahead.shape
    rows = atoms // steps
    block = pl.BlockSpec((rows, channels), lambda i: (i, 0))
    whole = pl.BlockSpec(own.shape, lambda i: (0, 0, 0), pipeline_mode=pl.Buffered(1))
    return pl.pallas_call(
        functools.partial(final_kernel, order),
        grid=(steps,),
        out_shape=(jax.ShapeDtypeStruct((atoms, channels), BF16),) * 2,
        in_specs=[
            SMEM,
            whole,
            whole,
            pl.BlockSpec((rows, table.shape[1]), lambda i: (i, 0)),
            block,
            block,
        ],
        out_specs=(block, block),
        scratch_shapes=[pltpu.VMEM((table.shape[1], 2 * channels), BF16)],
        compiler_params=pltpu.CompilerParams(vmem_limit_bytes=16 << 20),
        cost_estimate=pl.CostEstimate(flops=1 << 30, bytes_accessed=4 << 20, transcendentals=0),
        name="final",
    )(seat, own, other, table, ahead, mixed)


def order_of_tiles():
    out = []
    for tile in range(256):
        y, x, z_lo, z_hi = tile // 64, tile // 16 % 4, tile // 4 % 4, tile % 4
        out.append(((z_lo * 4 + y) * 4 + x) * 4 + z_hi)
    return tuple(out)


def body(
    embedding, cotangent, fractional, wave_index, tile_pairs, counts, wave_filter, short_weight
):
    devices = math.prod(lax.axis_size(name) for name in FINE)
    atoms_all = embedding.shape[0] * devices
    core, x, y = (lax.axis_index(name).astype(jnp.int32) for name in ("core", "x", "y"))
    z_lo, z_hi = lax.axis_index("z_lo").astype(jnp.int32), lax.axis_index("z_hi").astype(jnp.int32)
    seat = jnp.stack([core, core * 32 + (y & 1) * 16 + x * 4 + z_lo, z_hi & 1])
    swap = [(0, 1), (1, 0)]

    given = lax.ppermute(
        partial_sums(1 - seat[:1], wave_index, fractional, embedding, cotangent), "core", swap
    )
    kept = partial_sums(seat[:1], wave_index, fractional, embedding, cotangent)
    chip = lax.all_to_all(add(kept, given), ("y", "x"), 0, 0, tiled=True)
    embedding_above = shifted(embedding, -1)
    places_above = shifted(fractional, -1)
    table, scale = tables(seat, wave_index, fractional, wave_filter, atoms_all)
    summed = gather_sum(chip)
    parts = lax.all_to_all(summed, ALONG_Z, 0, 0, tiled=True)
    ahead, behind, behind_next = near(
        tile_pairs.reshape(-1), counts, embedding, embedding_above, cotangent, fractional, places_above,
        short_weight,
    )
    below = shifted(behind_next, 1)
    mixed = mixing(behind, below, short_weight)
    spread = coefficients(parts, scale)
    coeffs = lax.all_to_all(spread, FINE[:4], 0, 0, tiled=True)
    other = lax.ppermute(coeffs, "core", swap)
    return final(order_of_tiles(), seat, coeffs, other, table, ahead, mixed)


def shifted(value, by):
    size = math.prod(lax.axis_size(name) for name in FINE)
    return lax.ppermute(value, FINE, [(i, (i + by) % size) for i in range(size)])


def solution(mesh):
    fine = Mesh(mesh.devices.reshape(4, 4, 4, 4, 2), FINE)
    rows, places, one = P(FINE, None), P(None, FINE), P(FINE)
    return jax.shard_map(
        body,
        mesh=fine,
        in_specs=(rows, rows, places, P(), rows, one, P(), P()),
        out_specs=(rows, rows),
        check_vma=False,
    )
```

```python
import functools
import math

import jax
import jax.numpy as jnp
from jax import lax
from jax.experimental import pallas as pl
from jax.experimental.pallas import tpu as pltpu
from jax.sharding import Mesh
from jax.sharding import PartitionSpec as P


TILE = 128
FINE = ("z_lo", "y", "x", "z_hi", "core")
ALONG_Z = ("z_lo", "z_hi")
F32, BF16 = jnp.float32, jnp.bfloat16
VMEM = pl.BlockSpec(memory_space=pltpu.VMEM)
SMEM = pl.BlockSpec(memory_space=pltpu.SMEM)

COS = (
    0.9999999889445764,
    -19.73920446657614,
    64.93911592834654,
    -85.45011342750612,
    60.167429791960785,
    -25.966884612677454,
    6.527705963152031,
)
SIN = (
    6.283185302468581,
    -41.34170039298386,
    81.60513081114435,
    -76.70300555818746,
    42.02585148963868,
    -14.899578436725896,
    3.2377800860428168,
)


def cos_sin(turns):
    r = turns - jnp.floor(turns + 0.5)
    u = r * r
    c, s = COS[-1], SIN[-1]
    for k in COS[-2::-1]:
        c = c * u + k
    for k in SIN[-2::-1]:
        s = s * u + k
    return c, s * r


def dot(a, b, dims=((1,), (0,))):
    return lax.dot_general(a, b, (dims, ((), ())), preferred_element_type=F32)


def padded(rows):
    rows = rows.astype(F32)
    return jnp.concatenate([rows, jnp.zeros((5, rows.shape[1]), F32)], axis=0)


def sums_kernel(seat, waves_far, places_far, left_far, right_far, out, waves, places, left, right, turns, table, sems):
    half, atoms = turns.shape
    mine = pl.ds(pl.multiple_of(seat[0] * half, half), half)
    loads = [
        pltpu.make_async_copy(waves_far.at[:, mine], waves, sems.at[0]),
        pltpu.make_async_copy(places_far, places, sems.at[1]),
        pltpu.make_async_copy(left_far, left, sems.at[2]),
        pltpu.make_async_copy(right_far, right, sems.at[3]),
    ]
    for load in loads:
        load.start()
    loads[0].wait()
    loads[1].wait()
    turns[...] = dot(padded(waves[...]).astype(BF16), padded(places[...]).astype(BF16), ((0,), (0,)))

    @pl.loop(0, half // 16)
    def _(i):
        top = pl.ds(pl.multiple_of(i * 16, 16), 16)
        low = pl.ds(pl.multiple_of(half + i * 16, 16), 16)
        for j in range(atoms // 256):
            cols = pl.ds(j * 256, 256)
            c, s = cos_sin(turns[top, cols])
            table[top, cols] = c.astype(BF16)
            table[low, cols] = s.astype(BF16)

    for side, ref in enumerate((left, right)):
        loads[2 + side].wait()
        for block in range(2):
            part = dot(table[block * half : block * half + half, :], ref[...])
            for r in range(half // 8):
                i, k = divmod(block * (half // 8) + r, 4)
                for q in range(2):
                    out[i, k * 4 + side * 2 + q] = part[8 * r : 8 * r + 8, 128 * q : 128 * q + 128]


def partial_sums(seat, waves, places, left, right):
    half, atoms = waves.shape[1] // 2, places.shape[1]
    return pl.pallas_call(
        sums_kernel,
        out_shape=jax.ShapeDtypeStruct((16, 16, 8, 128), F32),
        in_specs=[SMEM] + [pl.BlockSpec(memory_space=pltpu.HBM)] * 4,
        out_specs=VMEM,
        scratch_shapes=[
            pltpu.VMEM((3, half), waves.dtype),
            pltpu.VMEM(places.shape, BF16),
            pltpu.VMEM(left.shape, BF16),
            pltpu.VMEM(right.shape, BF16),
            pltpu.VMEM((half, atoms), F32),
            pltpu.VMEM((2 * half, atoms), BF16),
            pltpu.SemaphoreType.DMA((4,)),
        ],
        compiler_params=pltpu.CompilerParams(vmem_limit_bytes=12 << 20),
        cost_estimate=pl.CostEstimate(
            flops=4 * half * atoms * 512, bytes_accessed=2 << 20, transcendentals=0
        ),
        name="sums",
    )(seat, *map(in_hbm, (waves, places, left, right)))


def add_kernel(a, b, out):
    @pl.loop(0, a.shape[0])
    def _(i):
        out[i] = a[i] + b[i]


def add(a, b):
    return pl.pallas_call(
        add_kernel,
        out_shape=jax.ShapeDtypeStruct(a.shape, F32),
        in_specs=[VMEM] * 2,
        out_specs=VMEM,
        compiler_params=pltpu.CompilerParams(vmem_limit_bytes=4 << 20),
        name="add",
    )(a, b)


def gather_sum_kernel(a, out):
    @pl.loop(0, out.shape[0])
    def _(i):
        total = a[0, i]
        for k in range(1, a.shape[0]):
            total = total + a[k, i]
        out[i] = total


def gather_sum(a):
    return pl.pallas_call(
        gather_sum_kernel,
        out_shape=jax.ShapeDtypeStruct(a.shape[1:], F32),
        in_specs=[VMEM],
        out_specs=VMEM,
        compiler_params=pltpu.CompilerParams(vmem_limit_bytes=4 << 20),
        name="plane_sum",
    )(a)


def coefficients_kernel(a, scale, out):
    total = a[0]
    for k in range(1, a.shape[0]):
        total = total + a[k]
    mine = (total * scale[...]).astype(BF16)

    @pl.loop(0, out.shape[0] // 8)
    def _(i):
        for k in range(8):
            out[i * 8 + k] = mine


def coefficients(a, scale):
    return pl.pallas_call(
        coefficients_kernel,
        out_shape=jax.ShapeDtypeStruct((256, 8, 128), BF16),
        in_specs=[VMEM] * 2,
        out_specs=VMEM,
        compiler_params=pltpu.CompilerParams(vmem_limit_bytes=4 << 20),
        name="coefficients",
    )(a, scale)


def table_kernel(seat, waves, places, wave_filter, table, scale, turns, *, atoms_all):
    atoms, count = turns.shape
    half = count // 2
    turns[...] = dot(padded(places[...]).astype(BF16), padded(waves[...]).astype(BF16), ((0,), (0,)))

    @pl.loop(0, atoms // 16)
    def _(i):
        rows = pl.ds(pl.multiple_of(i * 16, 16), 16)
        for j in range(2):
            c, s = cos_sin(turns[rows, j * half : j * half + half])
            table[rows, 2 * j * half : (2 * j + 1) * half] = c.astype(BF16)
            table[rows, (2 * j + 1) * half : (2 * j + 2) * half] = s.astype(BF16)

    row, col = seat[1], seat[2]
    tile = wave_filter[pl.ds(pl.multiple_of(row * 8, 8), 8), pl.ds(pl.multiple_of(col * 128, 128), 128)]
    scale[...] = tile * (1.0 / math.sqrt(atoms_all))


def tables(seat, waves, places, wave_filter, atoms_all):
    atoms, count = places.shape[1], waves.shape[1]
    return pl.pallas_call(
        functools.partial(table_kernel, atoms_all=atoms_all),
        out_shape=(
            jax.ShapeDtypeStruct((atoms, 2 * count), BF16),
            jax.ShapeDtypeStruct((8, 128), F32),
        ),
        in_specs=[SMEM] + [VMEM] * 3,
        out_specs=(VMEM, VMEM),
        scratch_shapes=[pltpu.VMEM((atoms, count), F32)],
        compiler_params=pltpu.CompilerParams(vmem_limit_bytes=12 << 20),
        cost_estimate=pl.CostEstimate(flops=6 << 30, bytes_accessed=2 << 20, transcendentals=0),
        name="table",
    )(seat, waves, places, wave_filter)


def thirds(value):
    a = value.astype(BF16).astype(F32)
    b = (value - a).astype(BF16).astype(F32)
    return a, b, value - a - b


def features(places):
    coords = padded(places)
    live = lax.broadcasted_iota(jnp.int32, coords.shape, 0) < 3
    parts = [thirds(jnp.where(live, v, 0.0)) for v in cos_sin(coords)]
    left = jnp.concatenate([p[k] for k in (0, 0, 1, 1, 0, 2) for p in parts], axis=0)
    right = jnp.concatenate([p[k] for k in (0, 1, 0, 1, 2, 0) for p in parts], axis=0)
    return left, right


PLACES, PAIRS, LIVE, ABOVE_ROWS, BELOW_ROWS = 1024, 1040, 1064, 1040, 1072


def pack_kernel(embedding, cotangent, places, pairs, count, above, below, sems):
    atoms = embedding.shape[0]
    loads = [
        pltpu.make_async_copy(embedding, above.at[pl.ds(0, atoms)], sems.at[0]),
        pltpu.make_async_copy(cotangent, below.at[pl.ds(0, atoms)], sems.at[1]),
    ]
    for load in loads:
        load.start()
    width = above.shape[1]
    coords = places[...].astype(F32)
    rows = [coords[d : d + 1, k * width : k * width + width] for d in range(3) for k in range(4)]
    rows = jnp.concatenate([*rows, jnp.zeros((4, width), F32)], axis=0).astype(BF16)
    above[PLACES : PLACES + 16, :] = rows
    below[PLACES : PLACES + 16, :] = rows
    tail = jnp.where(lax.broadcasted_iota(jnp.int32, (32, width), 0) >= LIVE - PAIRS, count[0], 0)
    below[PAIRS:BELOW_ROWS, :] = tail.astype(F32).astype(BF16)
    below[PAIRS:LIVE, 0:2] = pairs[...].astype(F32).astype(BF16)
    for load in loads:
        load.wait()


def pack(embedding, cotangent, places, pairs, count):
    width = embedding.shape[1]
    hbm = pl.BlockSpec(memory_space=pltpu.HBM)
    return pl.pallas_call(
        pack_kernel,
        out_shape=(
            jax.ShapeDtypeStruct((ABOVE_ROWS, width), BF16),
            jax.ShapeDtypeStruct((BELOW_ROWS, width), BF16),
        ),
        in_specs=[hbm, hbm, VMEM, VMEM, SMEM],
        out_specs=(VMEM, VMEM),
        scratch_shapes=[pltpu.SemaphoreType.DMA((2,))],
        compiler_params=pltpu.CompilerParams(vmem_limit_bytes=4 << 20),
        name="pack",
    )(in_hbm(embedding), in_hbm(cotangent), places, pairs, count)


def in_hbm(value):
    return pltpu.with_memory_space_constraint(value, pltpu.HBM)


GROUP = 4


def near_kernel(
    pairs, count, pairs_below, count_below, embedding, above, cotangent, below, places, weight,
    ahead, mixed,
    projected, back, lefts, lefts_below, rights, far_places,
):
    atoms, width = embedding.shape
    tiles = atoms // TILE
    projected[pl.ds(0, atoms), :] = dot(embedding[...], weight[...]).astype(BF16)
    projected[pl.ds(atoms, atoms), :] = dot(above[pl.ds(0, atoms), :], weight[...]).astype(BF16)
    for side, ref in enumerate((above, below)):
        rows = ref[PLACES : PLACES + 16, :].astype(F32)
        for d in range(3):
            for k in range(4):
                far_places[side, d : d + 1, k * width : k * width + width] = rows[4 * d + k : 4 * d + k + 1]
    left, right = features(places[...])
    _, right_above = features(far_places[0])
    left_below, _ = features(far_places[1])
    lefts[...] = left.T.astype(BF16)
    lefts_below[...] = left_below.T.astype(BF16)
    for t in range(tiles):
        cut = slice(t * TILE, t * TILE + TILE)
        rights[t] = right[:, cut].astype(BF16)
        rights[tiles + t] = right_above[:, cut].astype(BF16)
    ahead[...] = jnp.zeros_like(ahead)
    back[...] = jnp.zeros_like(back)
    shift = -3.0 - 0.5 * math.log(TILE)

    def rows_of(t):
        return pl.ds(pl.multiple_of(t * TILE, TILE), TILE)

    @pl.loop(0, pairs.shape[0] // (2 * GROUP))
    def _(g):
        fore, rear = [], []
        for j in range(GROUP):
            p = g * GROUP + j
            u, v = pairs[2 * p], pairs[2 * p + 1]
            k = jnp.exp(dot(lefts[rows_of(u), :], rights[v]) + shift)
            k = jnp.where(p < count[0], k, 0.0)
            fore.append((u, dot(k.astype(BF16), projected[rows_of(v), :])))
            k = jnp.where(v < tiles, k, 0.0)
            own = jnp.where(v < tiles, v, v - tiles)
            rear.append((own, dot(k.T.astype(BF16), cotangent[rows_of(u), :])))
            u, v = pairs_below[2 * p], pairs_below[2 * p + 1]
            own = jnp.where(v < tiles, v, v - tiles)
            k = jnp.exp(dot(lefts_below[rows_of(u), :], rights[own]) + shift)
            k = jnp.where((p < count_below[0]) & (v >= tiles), k, 0.0)
            rear.append((own, dot(k.T.astype(BF16), below[rows_of(u), :])))
        for t, part in fore:
            ahead[rows_of(t), :] += part
        for t, part in rear:
            back[rows_of(t), :] += part

    mixed[...] = dot(back[...].astype(BF16), weight[...], ((1,), (1,)))


def near(pairs, count, pairs_below, count_below, embedding, above, cotangent, below, places, weight):
    atoms, channels = embedding.shape
    tiles = atoms // TILE
    return pl.pallas_call(
        near_kernel,
        out_shape=(jax.ShapeDtypeStruct((atoms, channels), F32),) * 2,
        in_specs=[SMEM] * 4 + [VMEM] * 6,
        out_specs=(VMEM, VMEM),
        scratch_shapes=[
            pltpu.VMEM((2 * atoms, channels), BF16),
            pltpu.VMEM((atoms, channels), F32),
            pltpu.VMEM((atoms, 96), BF16),
            pltpu.VMEM((atoms, 96), BF16),
            pltpu.VMEM((2 * tiles, 96, TILE), BF16),
            pltpu.VMEM((2, 3, atoms), F32),
        ],
        compiler_params=pltpu.CompilerParams(vmem_limit_bytes=16 << 20),
        cost_estimate=pl.CostEstimate(flops=10 << 30, bytes_accessed=4 << 20, transcendentals=0),
        name="near",
    )(pairs, count, pairs_below, count_below, embedding, above, cotangent, below, places, weight)


def final_kernel(order, seat, own, other, table, ahead, mixed, message, grad, matrix):
    channels = message.shape[1]

    @pl.when(pl.program_id(0) == 0)
    def _():
        for half, ref in ((seat[0], own), (1 - seat[0], other)):
            for r in range(0, 64, 2):
                rows = pl.ds(pl.multiple_of(half * 512 + 8 * r, 16), 16)
                for q in range(4):
                    pair = [ref[order[(r + d) * 4 + q]].astype(F32) for d in range(2)]
                    matrix[rows, 128 * q : 128 * q + 128] = jnp.concatenate(pair, axis=0).astype(BF16)

    message[...] = (dot(table[...], matrix[:, :channels]) + ahead[...]).astype(BF16)
    grad[...] = (dot(table[...], matrix[:, channels:]) + mixed[...]).astype(BF16)


def final(order, seat, own, other, table, ahead, mixed, steps=4):
    atoms, channels = ahead.shape
    rows = atoms // steps
    block = pl.BlockSpec((rows, channels), lambda i: (i, 0))
    whole = pl.BlockSpec(own.shape, lambda i: (0, 0, 0), pipeline_mode=pl.Buffered(1))
    return pl.pallas_call(
        functools.partial(final_kernel, order),
        grid=(steps,),
        out_shape=(jax.ShapeDtypeStruct((atoms, channels), BF16),) * 2,
        in_specs=[
            SMEM,
            whole,
            whole,
            pl.BlockSpec((rows, table.shape[1]), lambda i: (i, 0)),
            block,
            block,
        ],
        out_specs=(block, block),
        scratch_shapes=[pltpu.VMEM((table.shape[1], 2 * channels), BF16)],
        compiler_params=pltpu.CompilerParams(vmem_limit_bytes=16 << 20),
        cost_estimate=pl.CostEstimate(flops=1 << 30, bytes_accessed=4 << 20, transcendentals=0),
        name="final",
    )(seat, own, other, *map(in_hbm, (table, ahead, mixed)))


def order_of_tiles():
    out = []
    for tile in range(256):
        y, x, z_lo, z_hi = tile // 64, tile // 16 % 4, tile // 4 % 4, tile % 4
        out.append(((z_lo * 4 + y) * 4 + x) * 4 + z_hi)
    return tuple(out)


def body(
    embedding, cotangent, fractional, wave_index, tile_pairs, counts, wave_filter, short_weight
):
    devices = math.prod(lax.axis_size(name) for name in FINE)
    atoms_all = embedding.shape[0] * devices
    core, x, y = (lax.axis_index(name).astype(jnp.int32) for name in ("core", "x", "y"))
    z_lo, z_hi = lax.axis_index("z_lo").astype(jnp.int32), lax.axis_index("z_hi").astype(jnp.int32)
    seat = jnp.stack([core, core * 32 + (y & 1) * 16 + x * 4 + z_lo, z_hi & 1])
    swap = [(0, 1), (1, 0)]

    to_above, to_below = pack(embedding, cotangent, fractional, tile_pairs, counts)
    above = shifted(to_above, -1)
    below = shifted(to_below, 1)
    given = partial_sums(1 - seat[:1], wave_index, fractional, embedding, cotangent)
    given = lax.ppermute(given, "core", swap)
    kept = partial_sums(seat[:1], wave_index, fractional, embedding, cotangent)
    total = add(kept, given)
    chip = lax.all_to_all(total, ("y", "x"), 0, 0, tiled=True)
    table, scale = tables(seat, wave_index, fractional, wave_filter, atoms_all)
    summed = gather_sum(chip)
    parts = lax.all_to_all(summed, ALONG_Z, 0, 0, tiled=True)
    spread = coefficients(parts, scale)
    coeffs = lax.all_to_all(spread, FINE[:4], 0, 0, tiled=True)
    pairs_below = below[PAIRS:LIVE, 0:2].astype(jnp.int32).reshape(-1)
    count_below = below[LIVE, 0:1].astype(jnp.int32)
    ahead, mixed = near(
        tile_pairs.reshape(-1), counts, pairs_below, count_below, embedding, above, cotangent, below,
        fractional, short_weight,
    )
    other = lax.ppermute(coeffs, "core", swap)
    return final(order_of_tiles(), seat, coeffs, other, table, ahead, mixed)


def shifted(value, by):
    size = math.prod(lax.axis_size(name) for name in FINE)
    return lax.ppermute(value, FINE, [(i, (i + by) % size) for i in range(size)])


def solution(mesh):
    fine = Mesh(mesh.devices.reshape(4, 4, 4, 4, 2), FINE)
    rows, places, one = P(FINE, None), P(None, FINE), P(FINE)
    return jax.shard_map(
        body,
        mesh=fine,
        in_specs=(rows, rows, places, P(), rows, one, P(), P()),
        out_specs=(rows, rows),
        check_vma=False,
    )
```

```python
import functools
import math

import jax
import jax.numpy as jnp
from jax import lax
from jax.experimental import pallas as pl
from jax.experimental.pallas import tpu as pltpu
from jax.sharding import Mesh
from jax.sharding import PartitionSpec as P


TILE = 128
FINE = ("z_lo", "y", "x", "z_hi", "core")
ALONG_Z = ("z_lo", "z_hi")
F32, BF16 = jnp.float32, jnp.bfloat16
VMEM = pl.BlockSpec(memory_space=pltpu.VMEM)
SMEM = pl.BlockSpec(memory_space=pltpu.SMEM)

COS = (
    0.9999999889445764,
    -19.73920446657614,
    64.93911592834654,
    -85.45011342750612,
    60.167429791960785,
    -25.966884612677454,
    6.527705963152031,
)
SIN = (
    6.283185302468581,
    -41.34170039298386,
    81.60513081114435,
    -76.70300555818746,
    42.02585148963868,
    -14.899578436725896,
    3.2377800860428168,
)


def cos_sin(turns):
    r = turns - jnp.floor(turns + 0.5)
    u = r * r
    c, s = COS[-1], SIN[-1]
    for k in COS[-2::-1]:
        c = c * u + k
    for k in SIN[-2::-1]:
        s = s * u + k
    return c, s * r


def dot(a, b, dims=((1,), (0,))):
    return lax.dot_general(a, b, (dims, ((), ())), preferred_element_type=F32)


def padded(rows):
    rows = rows.astype(F32)
    return jnp.concatenate([rows, jnp.zeros((5, rows.shape[1]), F32)], axis=0)


def sums_kernel(seat, waves_far, places_far, left_far, right_far, out, waves, places, left, right, turns, table, sems):
    half, atoms = turns.shape
    mine = pl.ds(pl.multiple_of(seat[0] * half, half), half)
    loads = [
        pltpu.make_async_copy(waves_far.at[:, mine], waves, sems.at[0]),
        pltpu.make_async_copy(places_far, places, sems.at[1]),
        pltpu.make_async_copy(left_far, left, sems.at[2]),
        pltpu.make_async_copy(right_far, right, sems.at[3]),
    ]
    for load in loads:
        load.start()
    loads[0].wait()
    loads[1].wait()
    turns[...] = dot(padded(waves[...]).astype(BF16), padded(places[...]).astype(BF16), ((0,), (0,)))

    @pl.loop(0, half // 16)
    def _(i):
        top = pl.ds(pl.multiple_of(i * 16, 16), 16)
        low = pl.ds(pl.multiple_of(half + i * 16, 16), 16)
        for j in range(atoms // 256):
            cols = pl.ds(j * 256, 256)
            c, s = cos_sin(turns[top, cols])
            table[top, cols] = c.astype(BF16)
            table[low, cols] = s.astype(BF16)

    for side, ref in enumerate((left, right)):
        loads[2 + side].wait()
        for block in range(2):
            part = dot(table[block * half : block * half + half, :], ref[...])
            for r in range(half // 8):
                i, k = divmod(block * (half // 8) + r, 4)
                for q in range(2):
                    out[i, k * 4 + side * 2 + q] = part[8 * r : 8 * r + 8, 128 * q : 128 * q + 128]


def partial_sums(seat, waves, places, left, right):
    half, atoms = waves.shape[1] // 2, places.shape[1]
    return pl.pallas_call(
        sums_kernel,
        out_shape=jax.ShapeDtypeStruct((16, 16, 8, 128), F32),
        in_specs=[SMEM] + [pl.BlockSpec(memory_space=pltpu.HBM)] * 4,
        out_specs=VMEM,
        scratch_shapes=[
            pltpu.VMEM((3, half), waves.dtype),
            pltpu.VMEM(places.shape, BF16),
            pltpu.VMEM(left.shape, BF16),
            pltpu.VMEM(right.shape, BF16),
            pltpu.VMEM((half, atoms), F32),
            pltpu.VMEM((2 * half, atoms), BF16),
            pltpu.SemaphoreType.DMA((4,)),
        ],
        compiler_params=pltpu.CompilerParams(vmem_limit_bytes=12 << 20),
        cost_estimate=pl.CostEstimate(
            flops=4 * half * atoms * 512, bytes_accessed=2 << 20, transcendentals=0
        ),
        name="sums",
    )(seat, *map(in_hbm, (waves, places, left, right)))


def add_kernel(a, b, out):
    @pl.loop(0, a.shape[0])
    def _(i):
        out[i] = a[i] + b[i]


def add(a, b):
    return pl.pallas_call(
        add_kernel,
        out_shape=jax.ShapeDtypeStruct(a.shape, F32),
        in_specs=[VMEM] * 2,
        out_specs=VMEM,
        compiler_params=pltpu.CompilerParams(vmem_limit_bytes=4 << 20),
        name="add",
    )(a, b)


def gather_sum_kernel(a, out):
    @pl.loop(0, out.shape[0])
    def _(i):
        total = a[0, i]
        for k in range(1, a.shape[0]):
            total = total + a[k, i]
        out[i] = total


def gather_sum(a):
    return pl.pallas_call(
        gather_sum_kernel,
        out_shape=jax.ShapeDtypeStruct(a.shape[1:], F32),
        in_specs=[VMEM],
        out_specs=VMEM,
        compiler_params=pltpu.CompilerParams(vmem_limit_bytes=4 << 20),
        name="plane_sum",
    )(a)


def coefficients_kernel(a, scale, out):
    total = a[0]
    for k in range(1, a.shape[0]):
        total = total + a[k]
    mine = (total * scale[...]).astype(BF16)
    for k in range(out.shape[0]):
        out[k] = mine


def coefficients(a, scale):
    return pl.pallas_call(
        coefficients_kernel,
        out_shape=jax.ShapeDtypeStruct(a.shape, BF16),
        in_specs=[VMEM] * 2,
        out_specs=VMEM,
        compiler_params=pltpu.CompilerParams(vmem_limit_bytes=4 << 20),
        name="coefficients",
    )(a, scale)


def copies_kernel(a, out):
    for k in range(a.shape[0]):
        mine = a[k]

        @pl.loop(0, out.shape[0], unroll=True)
        def _(i):
            out[i, k] = mine


def copies(a):
    return pl.pallas_call(
        copies_kernel,
        out_shape=jax.ShapeDtypeStruct((16, *a.shape), BF16),
        in_specs=[VMEM],
        out_specs=VMEM,
        compiler_params=pltpu.CompilerParams(vmem_limit_bytes=4 << 20),
        name="copies",
    )(a)


def table_kernel(seat, waves, places, wave_filter, table, scale, turns, *, atoms_all):
    atoms, count = turns.shape
    half = count // 2
    turns[...] = dot(padded(places[...]).astype(BF16), padded(waves[...]).astype(BF16), ((0,), (0,)))

    @pl.loop(0, atoms // 16)
    def _(i):
        rows = pl.ds(pl.multiple_of(i * 16, 16), 16)
        for j in range(2):
            c, s = cos_sin(turns[rows, j * half : j * half + half])
            table[rows, 2 * j * half : (2 * j + 1) * half] = c.astype(BF16)
            table[rows, (2 * j + 1) * half : (2 * j + 2) * half] = s.astype(BF16)

    row, col = seat[1], seat[2]
    tile = wave_filter[pl.ds(pl.multiple_of(row * 8, 8), 8), pl.ds(pl.multiple_of(col * 128, 128), 128)]
    scale[...] = tile * (1.0 / math.sqrt(atoms_all))


def tables(seat, waves, places, wave_filter, atoms_all):
    atoms, count = places.shape[1], waves.shape[1]
    return pl.pallas_call(
        functools.partial(table_kernel, atoms_all=atoms_all),
        out_shape=(
            jax.ShapeDtypeStruct((atoms, 2 * count), BF16),
            jax.ShapeDtypeStruct((8, 128), F32),
        ),
        in_specs=[SMEM] + [VMEM] * 3,
        out_specs=(VMEM, VMEM),
        scratch_shapes=[pltpu.VMEM((atoms, count), F32)],
        compiler_params=pltpu.CompilerParams(vmem_limit_bytes=12 << 20),
        cost_estimate=pl.CostEstimate(flops=6 << 30, bytes_accessed=2 << 20, transcendentals=0),
        name="table",
    )(seat, waves, places, wave_filter)


def thirds(value):
    a = value.astype(BF16).astype(F32)
    b = (value - a).astype(BF16).astype(F32)
    return a, b, value - a - b


def features(places):
    coords = padded(places)
    live = lax.broadcasted_iota(jnp.int32, coords.shape, 0) < 3
    parts = [thirds(jnp.where(live, v, 0.0)) for v in cos_sin(coords)]
    left = jnp.concatenate([p[k] for k in (0, 0, 1, 1, 0, 2) for p in parts], axis=0)
    right = jnp.concatenate([p[k] for k in (0, 1, 0, 1, 2, 0) for p in parts], axis=0)
    return left, right


PLACES, PAIRS, LIVE, ROWS = 1024, 1040, 1048, 1056


def pack_kernel(seat, embedding, cotangent, places_far, pairs, count, far, close, places, sems):
    atoms = embedding.shape[0]
    positions = pltpu.make_async_copy(places_far, places, sems.at[2])
    positions.start()

    def both(forward, backward):
        a = pltpu.make_async_copy(embedding, backward.at[pl.ds(0, atoms)], sems.at[0])
        b = pltpu.make_async_copy(cotangent, forward.at[pl.ds(0, atoms)], sems.at[1])
        a.start()
        b.start()
        return a, b

    @pl.when(seat[0] == 0)
    def _():
        both(close, far)

    @pl.when(seat[0] != 0)
    def _():
        both(far, close)

    width = far.shape[1]
    positions.wait()
    coords = places[...].astype(F32)
    rows = [coords[d : d + 1, k * width : k * width + width] for d in range(3) for k in range(4)]
    rows = jnp.concatenate([*rows, jnp.zeros((4, width), F32)], axis=0).astype(BF16)
    listed = jnp.concatenate([pairs[...].astype(F32), jnp.zeros((2, width - pairs.shape[1]), F32)], axis=1)
    listed = jnp.concatenate([listed, jnp.zeros((6, width), F32)], axis=0)
    tail = jnp.concatenate([listed, jnp.full((8, width), count[0], jnp.int32).astype(F32)], axis=0).astype(BF16)
    for ref in (far, close):
        ref[PLACES:PAIRS, :] = rows
        ref[PAIRS:ROWS, :] = tail
    pltpu.make_async_copy(embedding, far.at[pl.ds(0, atoms)], sems.at[0]).wait()
    pltpu.make_async_copy(cotangent, close.at[pl.ds(0, atoms)], sems.at[1]).wait()


def pack(seat, embedding, cotangent, places, pairs, count):
    hbm = pl.BlockSpec(memory_space=pltpu.HBM)
    return pl.pallas_call(
        pack_kernel,
        out_shape=(jax.ShapeDtypeStruct((ROWS, embedding.shape[1]), BF16),) * 2,
        in_specs=[SMEM, hbm, hbm, hbm, VMEM, SMEM],
        out_specs=(VMEM, VMEM),
        scratch_shapes=[pltpu.VMEM(places.shape, BF16), pltpu.SemaphoreType.DMA((3,))],
        compiler_params=pltpu.CompilerParams(vmem_limit_bytes=4 << 20),
        name="pack",
    )(seat, *map(in_hbm, (embedding, cotangent, places)), pairs, count)


def in_hbm(value):
    return pltpu.with_memory_space_constraint(value, pltpu.HBM)


GROUP = 4


def near_kernel(
    seat, pairs, count, pairs_below, count_below, embedding, cotangent, far, close, places, weight,
    ahead, mixed,
    around, projected, back, lefts, lefts_below, rights, far_places, sems,
):
    atoms, width = embedding.shape
    tiles = atoms // TILE
    loads = [
        pltpu.make_async_copy(close, around.at[seat[0]], sems.at[0]),
        pltpu.make_async_copy(far, around.at[1 - seat[0]], sems.at[1]),
    ]
    for load in loads:
        load.start()
    projected[pl.ds(0, atoms), :] = dot(embedding[...], weight[...]).astype(BF16)
    for load in loads:
        load.wait()
    above, below = around.at[0], around.at[1]
    projected[pl.ds(atoms, atoms), :] = dot(above[pl.ds(0, atoms), :], weight[...]).astype(BF16)
    for side, ref in enumerate((above, below)):
        rows = ref[PLACES:PAIRS, :].astype(F32)
        for d in range(3):
            for k in range(4):
                far_places[side, d : d + 1, k * width : k * width + width] = rows[4 * d + k : 4 * d + k + 1]
    left, right = features(places[...])
    _, right_above = features(far_places[0])
    left_below, _ = features(far_places[1])
    lefts[...] = left.T.astype(BF16)
    lefts_below[...] = left_below.T.astype(BF16)
    for t in range(tiles):
        cut = slice(t * TILE, t * TILE + TILE)
        rights[t] = right[:, cut].astype(BF16)
        rights[tiles + t] = right_above[:, cut].astype(BF16)
    ahead[...] = jnp.zeros_like(ahead)
    back[...] = jnp.zeros_like(back)
    shift = -3.0 - 0.5 * math.log(TILE)

    def rows_of(t):
        return pl.ds(pl.multiple_of(t * TILE, TILE), TILE)

    @pl.loop(0, pairs.shape[1] // GROUP)
    def _(g):
        fore, rear = [], []
        for j in range(GROUP):
            p = g * GROUP + j
            u, v = pairs[0, p], pairs[1, p]
            k = jnp.exp(dot(lefts[rows_of(u), :], rights[v]) + shift)
            k = jnp.where(p < count[0], k, 0.0)
            fore.append((u, dot(k.astype(BF16), projected[rows_of(v), :])))
            k = jnp.where(v < tiles, k, 0.0)
            own = jnp.where(v < tiles, v, v - tiles)
            rear.append((own, dot(k.T.astype(BF16), cotangent[rows_of(u), :])))
            u, v = pairs_below[0, p], pairs_below[1, p]
            own = jnp.where(v < tiles, v, v - tiles)
            k = jnp.exp(dot(lefts_below[rows_of(u), :], rights[own]) + shift)
            k = jnp.where((p < count_below[0]) & (v >= tiles), k, 0.0)
            rear.append((own, dot(k.T.astype(BF16), below[rows_of(u), :])))
        for t, part in fore:
            ahead[rows_of(t), :] += part
        for t, part in rear:
            back[rows_of(t), :] += part

    mixed[...] = dot(back[...].astype(BF16), weight[...], ((1,), (1,)))


def near(seat, pairs, count, pairs_below, count_below, embedding, cotangent, far, close, places, weight):
    atoms, channels = embedding.shape
    tiles = atoms // TILE
    hbm = pl.BlockSpec(memory_space=pltpu.HBM)
    return pl.pallas_call(
        near_kernel,
        out_shape=(jax.ShapeDtypeStruct((atoms, channels), F32),) * 2,
        in_specs=[SMEM] * 5 + [VMEM] * 2 + [hbm] * 2 + [VMEM] * 2,
        out_specs=(VMEM, VMEM),
        scratch_shapes=[
            pltpu.VMEM((2, ROWS, channels), BF16),
            pltpu.VMEM((2 * atoms, channels), BF16),
            pltpu.VMEM((atoms, channels), F32),
            pltpu.VMEM((atoms, 96), BF16),
            pltpu.VMEM((atoms, 96), BF16),
            pltpu.VMEM((2 * tiles, 96, TILE), BF16),
            pltpu.VMEM((2, 3, atoms), F32),
            pltpu.SemaphoreType.DMA((2,)),
        ],
        compiler_params=pltpu.CompilerParams(vmem_limit_bytes=16 << 20),
        cost_estimate=pl.CostEstimate(flops=10 << 30, bytes_accessed=4 << 20, transcendentals=0),
        name="near",
    )(
        seat, pairs, count, pairs_below, count_below, embedding, cotangent, in_hbm(far), in_hbm(close), places, weight
    )


def final_kernel(seat, own, other, table, ahead, mixed, message, grad, matrix):
    channels = message.shape[1]

    @pl.when(pl.program_id(0) == 0)
    def _():
        for half, ref in ((seat[0], own), (1 - seat[0], other)):
            for r in range(0, 64, 2):
                rows = pl.ds(pl.multiple_of(half * 512 + 8 * r, 16), 16)
                for q in range(4):
                    pair = [ref[(r + d) * 4 + q].astype(F32) for d in range(2)]
                    matrix[rows, 128 * q : 128 * q + 128] = jnp.concatenate(pair, axis=0).astype(BF16)

    message[...] = (dot(table[...], matrix[:, :channels]) + ahead[...]).astype(BF16)
    grad[...] = (dot(table[...], matrix[:, channels:]) + mixed[...]).astype(BF16)


def final(seat, own, other, table, ahead, mixed, steps=4):
    atoms, channels = ahead.shape
    rows = atoms // steps
    block = pl.BlockSpec((rows, channels), lambda i: (i, 0))
    whole = pl.BlockSpec(own.shape, lambda i: (0, 0, 0), pipeline_mode=pl.Buffered(1))
    return pl.pallas_call(
        final_kernel,
        grid=(steps,),
        out_shape=(jax.ShapeDtypeStruct((atoms, channels), BF16),) * 2,
        in_specs=[
            SMEM,
            whole,
            whole,
            pl.BlockSpec((rows, table.shape[1]), lambda i: (i, 0)),
            block,
            block,
        ],
        out_specs=(block, block),
        scratch_shapes=[pltpu.VMEM((table.shape[1], 2 * channels), BF16)],
        compiler_params=pltpu.CompilerParams(vmem_limit_bytes=16 << 20),
        cost_estimate=pl.CostEstimate(flops=1 << 30, bytes_accessed=4 << 20, transcendentals=0),
        name="final",
    )(seat, own, other, *map(in_hbm, (table, ahead, mixed)))


def body(
    embedding, cotangent, fractional, wave_index, tile_pairs, counts, wave_filter, short_weight
):
    devices = math.prod(lax.axis_size(name) for name in FINE)
    atoms_all = embedding.shape[0] * devices
    core, x, y = (lax.axis_index(name).astype(jnp.int32) for name in ("core", "x", "y"))
    z_lo, z_hi = lax.axis_index("z_lo").astype(jnp.int32), lax.axis_index("z_hi").astype(jnp.int32)
    seat = jnp.stack([core, core * 32 + (y & 1) * 16 + x * 4 + z_lo, z_hi & 1])
    swap = [(0, 1), (1, 0)]

    listed = tile_pairs.T
    to_far, to_close = pack(seat[:1], embedding, cotangent, fractional, listed, counts)
    size = math.prod(lax.axis_size(name) for name in FINE)
    far = lax.ppermute(to_far, FINE, [(i, (i + (1 if i % 2 else -1)) % size) for i in range(size)])
    given = partial_sums(1 - seat[:1], wave_index, fractional, embedding, cotangent)
    given = lax.ppermute(given, "core", swap)
    kept = partial_sums(seat[:1], wave_index, fractional, embedding, cotangent)
    total = add(kept, given)
    chip = lax.all_to_all(total, ("y", "x"), 0, 0, tiled=True)
    close = lax.ppermute(to_close, "core", swap)
    table, scale = tables(seat, wave_index, fractional, wave_filter, atoms_all)
    summed = gather_sum(chip)
    parts = lax.all_to_all(summed, ALONG_Z, 0, 0, tiled=True)
    tail = jnp.where(seat[0] == 0, far[PAIRS:ROWS, :TILE], close[PAIRS:ROWS, :TILE]).astype(jnp.int32)
    pairs_below, count_below = tail[0:2, : listed.shape[1]], tail[LIVE - PAIRS, 0:1]
    mine = lax.all_to_all(coefficients(parts, scale), ALONG_Z, 0, 0, tiled=True)
    ahead, mixed = near(
        seat[:1], listed, counts, pairs_below, count_below, embedding, cotangent, far, close, fractional,
        short_weight,
    )
    coeffs = lax.all_to_all(copies(mine), ("y", "x"), 0, 0, tiled=True).reshape(256, 8, 128)
    other = lax.ppermute(coeffs, "core", swap)
    return final(seat, coeffs, other, table, ahead, mixed)


def solution(mesh):
    fine = Mesh(mesh.devices.reshape(4, 4, 4, 4, 2), FINE)
    rows, places, one = P(FINE, None), P(None, FINE), P(FINE)
    return jax.shard_map(
        body,
        mesh=fine,
        in_specs=(rows, rows, places, P(), rows, one, P(), P()),
        out_specs=(rows, rows),
        check_vma=False,
    )
```

```python
import functools
import math

import jax
import jax.numpy as jnp
from jax import lax
from jax.experimental import pallas as pl
from jax.experimental.pallas import tpu as pltpu
from jax.sharding import Mesh
from jax.sharding import PartitionSpec as P


TILE = 128
FINE = ("z_lo", "y", "x", "z_hi", "core")
ALONG_Z = ("z_lo", "z_hi")
F32, BF16 = jnp.float32, jnp.bfloat16
VMEM = pl.BlockSpec(memory_space=pltpu.VMEM)
SMEM = pl.BlockSpec(memory_space=pltpu.SMEM)

COS = (
    0.9999999889445764,
    -19.73920446657614,
    64.93911592834654,
    -85.45011342750612,
    60.167429791960785,
    -25.966884612677454,
    6.527705963152031,
)
SIN = (
    6.283185302468581,
    -41.34170039298386,
    81.60513081114435,
    -76.70300555818746,
    42.02585148963868,
    -14.899578436725896,
    3.2377800860428168,
)


def cos_sin(turns):
    r = turns - jnp.floor(turns + 0.5)
    u = r * r
    c, s = COS[-1], SIN[-1]
    for k in COS[-2::-1]:
        c = c * u + k
    for k in SIN[-2::-1]:
        s = s * u + k
    return c, s * r


def dot(a, b, dims=((1,), (0,))):
    return lax.dot_general(a, b, (dims, ((), ())), preferred_element_type=F32)


def padded(rows):
    rows = rows.astype(F32)
    return jnp.concatenate([rows, jnp.zeros((5, rows.shape[1]), F32)], axis=0)


def sums_kernel(seat, waves_far, places_far, left_far, right_far, out, waves, places, left, right, turns, table, sems):
    half, atoms = turns.shape
    mine = pl.ds(pl.multiple_of(seat[0] * half, half), half)
    loads = [
        pltpu.make_async_copy(waves_far.at[:, mine], waves, sems.at[0]),
        pltpu.make_async_copy(places_far, places, sems.at[1]),
        pltpu.make_async_copy(left_far, left, sems.at[2]),
        pltpu.make_async_copy(right_far, right, sems.at[3]),
    ]
    for load in loads:
        load.start()
    loads[0].wait()
    loads[1].wait()
    turns[...] = dot(padded(waves[...]).astype(BF16), padded(places[...]).astype(BF16), ((0,), (0,)))

    @pl.loop(0, half // 16)
    def _(i):
        top = pl.ds(pl.multiple_of(i * 16, 16), 16)
        low = pl.ds(pl.multiple_of(half + i * 16, 16), 16)
        for j in range(atoms // 256):
            cols = pl.ds(j * 256, 256)
            c, s = cos_sin(turns[top, cols])
            table[top, cols] = c.astype(BF16)
            table[low, cols] = s.astype(BF16)

    for side, ref in enumerate((left, right)):
        loads[2 + side].wait()
        for block in range(2):
            part = dot(table[block * half : block * half + half, :], ref[...])
            for r in range(half // 8):
                i, k = divmod(block * (half // 8) + r, 4)
                for q in range(2):
                    out[i, k * 4 + side * 2 + q] = part[8 * r : 8 * r + 8, 128 * q : 128 * q + 128]


def partial_sums(seat, waves, places, left, right, first):
    half, atoms = waves.shape[1] // 2, places.shape[1]
    return pl.pallas_call(
        sums_kernel,
        out_shape=jax.ShapeDtypeStruct((16, 16, 8, 128), F32),
        in_specs=[SMEM] + [pl.BlockSpec(memory_space=pl.ANY)] * 4,
        out_specs=VMEM,
        scratch_shapes=[
            pltpu.VMEM((3, half), waves.dtype),
            pltpu.VMEM(places.shape, BF16),
            pltpu.VMEM(left.shape, BF16),
            pltpu.VMEM(right.shape, BF16),
            pltpu.VMEM((half, atoms), F32),
            pltpu.VMEM((2 * half, atoms), BF16),
            pltpu.SemaphoreType.DMA((4,)),
        ],
        compiler_params=pltpu.CompilerParams(vmem_limit_bytes=12 << 20),
        cost_estimate=pl.CostEstimate(
            flops=4 * half * atoms * 512, bytes_accessed=2 << 20, transcendentals=0
        ),
        name="sums",
    )(seat, *(map(in_hbm, (waves, places)) if first else (waves, places)), in_hbm(left), in_hbm(right))


def add_kernel(a, b, out):
    @pl.loop(0, a.shape[0])
    def _(i):
        out[i] = (a[i] + b[i]).astype(BF16)


def add(a, b):
    return pl.pallas_call(
        add_kernel,
        out_shape=jax.ShapeDtypeStruct(a.shape, BF16),
        in_specs=[VMEM] * 2,
        out_specs=VMEM,
        compiler_params=pltpu.CompilerParams(vmem_limit_bytes=4 << 20),
        name="add",
    )(a, b)


def gather_sum_kernel(a, out):
    @pl.loop(0, out.shape[0])
    def _(i):
        total = a[0, i].astype(F32)
        for k in range(1, a.shape[0]):
            total = total + a[k, i].astype(F32)
        out[i] = total


def gather_sum(a):
    return pl.pallas_call(
        gather_sum_kernel,
        out_shape=jax.ShapeDtypeStruct(a.shape[1:], F32),
        in_specs=[VMEM],
        out_specs=VMEM,
        compiler_params=pltpu.CompilerParams(vmem_limit_bytes=4 << 20),
        name="plane_sum",
    )(a)


def coefficients_kernel(a, scale, out):
    total = a[0]
    for k in range(1, a.shape[0]):
        total = total + a[k]
    mine = (total * scale[...]).astype(BF16)
    for k in range(out.shape[0]):
        out[k] = mine


def coefficients(a, scale):
    return pl.pallas_call(
        coefficients_kernel,
        out_shape=jax.ShapeDtypeStruct(a.shape, BF16),
        in_specs=[VMEM] * 2,
        out_specs=VMEM,
        compiler_params=pltpu.CompilerParams(vmem_limit_bytes=4 << 20),
        name="coefficients",
    )(a, scale)


def copies_kernel(a, out):
    for k in range(a.shape[0]):
        mine = a[k]

        @pl.loop(0, out.shape[0], unroll=True)
        def _(i):
            out[i, k] = mine


def copies(a):
    return pl.pallas_call(
        copies_kernel,
        out_shape=jax.ShapeDtypeStruct((16, *a.shape), BF16),
        in_specs=[VMEM],
        out_specs=VMEM,
        compiler_params=pltpu.CompilerParams(vmem_limit_bytes=4 << 20),
        name="copies",
    )(a)


def table_kernel(seat, waves, places, wave_filter, table, scale, turns, *, atoms_all):
    atoms, count = turns.shape
    half = count // 2
    turns[...] = dot(padded(places[...]).astype(BF16), padded(waves[...]).astype(BF16), ((0,), (0,)))

    @pl.loop(0, atoms // 16)
    def _(i):
        rows = pl.ds(pl.multiple_of(i * 16, 16), 16)
        for j in range(2):
            c, s = cos_sin(turns[rows, j * half : j * half + half])
            table[rows, 2 * j * half : (2 * j + 1) * half] = c.astype(BF16)
            table[rows, (2 * j + 1) * half : (2 * j + 2) * half] = s.astype(BF16)

    row, col = seat[1], seat[2]
    tile = wave_filter[pl.ds(pl.multiple_of(row * 8, 8), 8), pl.ds(pl.multiple_of(col * 128, 128), 128)]
    scale[...] = tile * (1.0 / math.sqrt(atoms_all))


def tables(seat, waves, places, wave_filter, atoms_all):
    atoms, count = places.shape[1], waves.shape[1]
    return pl.pallas_call(
        functools.partial(table_kernel, atoms_all=atoms_all),
        out_shape=(
            jax.ShapeDtypeStruct((atoms, 2 * count), BF16),
            jax.ShapeDtypeStruct((8, 128), F32),
        ),
        in_specs=[SMEM] + [VMEM] * 3,
        out_specs=(VMEM, VMEM),
        scratch_shapes=[pltpu.VMEM((atoms, count), F32)],
        compiler_params=pltpu.CompilerParams(vmem_limit_bytes=12 << 20),
        cost_estimate=pl.CostEstimate(flops=6 << 30, bytes_accessed=2 << 20, transcendentals=0),
        name="table",
    )(seat, waves, places, wave_filter)


def thirds(value):
    a = value.astype(BF16).astype(F32)
    b = (value - a).astype(BF16).astype(F32)
    return a, b, value - a - b


def features(places):
    coords = padded(places)
    live = lax.broadcasted_iota(jnp.int32, coords.shape, 0) < 3
    parts = [thirds(jnp.where(live, v, 0.0)) for v in cos_sin(coords)]
    left = jnp.concatenate([p[k] for k in (0, 0, 1, 1, 0, 2) for p in parts], axis=0)
    right = jnp.concatenate([p[k] for k in (0, 1, 0, 1, 2, 0) for p in parts], axis=0)
    return left, right


PLACES, PAIRS, LIVE, ROWS = 1024, 1040, 1048, 1056


def pack_kernel(seat, embedding, cotangent, places_far, pairs_far, count, far, close, places, pairs, sems):
    atoms = embedding.shape[0]
    small = [
        pltpu.make_async_copy(places_far, places, sems.at[2]),
        pltpu.make_async_copy(pairs_far, pairs, sems.at[3]),
    ]
    for load in small:
        load.start()

    def both(forward, backward):
        a = pltpu.make_async_copy(embedding, backward.at[pl.ds(0, atoms)], sems.at[0])
        b = pltpu.make_async_copy(cotangent, forward.at[pl.ds(0, atoms)], sems.at[1])
        a.start()
        b.start()
        return a, b

    @pl.when(seat[0] == 0)
    def _():
        both(close, far)

    @pl.when(seat[0] != 0)
    def _():
        both(far, close)

    width = far.shape[1]
    for load in small:
        load.wait()
    coords = places[...].astype(F32)
    rows = [coords[d : d + 1, k * width : k * width + width] for d in range(3) for k in range(4)]
    rows = jnp.concatenate([*rows, jnp.zeros((4, width), F32)], axis=0).astype(BF16)
    listed = jnp.concatenate([pairs[...].astype(F32), jnp.zeros((2, width - pairs.shape[1]), F32)], axis=1)
    listed = jnp.concatenate([listed, jnp.zeros((6, width), F32)], axis=0)
    tail = jnp.concatenate([listed, jnp.full((8, width), count[0], jnp.int32).astype(F32)], axis=0).astype(BF16)
    for ref in (far, close):
        ref[PLACES:PAIRS, :] = rows
        ref[PAIRS:ROWS, :] = tail
    pltpu.make_async_copy(embedding, far.at[pl.ds(0, atoms)], sems.at[0]).wait()
    pltpu.make_async_copy(cotangent, close.at[pl.ds(0, atoms)], sems.at[1]).wait()


def pack(seat, embedding, cotangent, places, pairs, count):
    hbm = pl.BlockSpec(memory_space=pltpu.HBM)
    return pl.pallas_call(
        pack_kernel,
        out_shape=(jax.ShapeDtypeStruct((ROWS, embedding.shape[1]), BF16),) * 2,
        in_specs=[SMEM, hbm, hbm, hbm, hbm, SMEM],
        out_specs=(VMEM, VMEM),
        scratch_shapes=[
            pltpu.VMEM(places.shape, BF16),
            pltpu.VMEM(pairs.shape, pairs.dtype),
            pltpu.SemaphoreType.DMA((4,)),
        ],
        compiler_params=pltpu.CompilerParams(vmem_limit_bytes=4 << 20),
        name="pack",
    )(seat, *map(in_hbm, (embedding, cotangent, places, pairs)), count)


def in_hbm(value):
    return pltpu.with_memory_space_constraint(value, pltpu.HBM)


GROUP = 4
SHIFT = -3.0 - 0.5 * math.log(TILE)


def rows_of(t):
    return pl.ds(pl.multiple_of(t * TILE, TILE), TILE)


def unpack_places(packed, places):
    width = packed.shape[1]
    rows = packed[PLACES:PAIRS, :].astype(F32)
    for d in range(3):
        for k in range(4):
            places[d : d + 1, k * width : k * width + width] = rows[4 * d + k : 4 * d + k + 1]


def store_tiles(rights, first, right):
    for t in range(right.shape[1] // TILE):
        rights[first + t] = right[:, t * TILE : t * TILE + TILE].astype(BF16)


def ahead_kernel(
    seat, pairs, count, embedding, far, close, places, weight, ahead, above, projected, lefts, rights, far_places, sem
):
    atoms = embedding.shape[0]

    @pl.when(seat[0] == 0)
    def _():
        pltpu.make_async_copy(close, above, sem).start()

    @pl.when(seat[0] != 0)
    def _():
        pltpu.make_async_copy(far, above, sem).start()

    projected[pl.ds(0, atoms), :] = dot(embedding[...], weight[...]).astype(BF16)
    left, right = features(places[...])
    lefts[...] = left.T.astype(BF16)
    store_tiles(rights, 0, right)
    ahead[...] = jnp.zeros_like(ahead)
    pltpu.make_async_copy(far, above, sem).wait()
    projected[pl.ds(atoms, atoms), :] = dot(above[pl.ds(0, atoms), :], weight[...]).astype(BF16)
    unpack_places(above, far_places)
    _, right = features(far_places[...])
    store_tiles(rights, atoms // TILE, right)

    @pl.loop(0, pairs.shape[1] // GROUP)
    def _(g):
        parts = []
        for j in range(GROUP):
            p = g * GROUP + j
            u, v = pairs[0, p], pairs[1, p]
            k = jnp.exp(dot(lefts[rows_of(u), :], rights[v]) + SHIFT)
            k = jnp.where(p < count[0], k, 0.0).astype(BF16)
            parts.append((u, dot(k, projected[rows_of(v), :])))
        for t, part in parts:
            ahead[rows_of(t), :] += part


def behind_kernel(
    seat, pairs, count, pairs_below, count_below, cotangent, far, close, places, weight,
    mixed,
    below, back, lefts, lefts_below, rights, far_places, sem,
):
    atoms = cotangent.shape[0]
    tiles = atoms // TILE

    @pl.when(seat[0] == 0)
    def _():
        pltpu.make_async_copy(far, below, sem).start()

    @pl.when(seat[0] != 0)
    def _():
        pltpu.make_async_copy(close, below, sem).start()

    left, right = features(places[...])
    lefts[...] = left.T.astype(BF16)
    store_tiles(rights, 0, right)
    back[...] = jnp.zeros_like(back)
    pltpu.make_async_copy(far, below, sem).wait()
    unpack_places(below, far_places)
    left, _ = features(far_places[...])
    lefts_below[...] = left.T.astype(BF16)

    def own_of(v):
        return jnp.where(v < tiles, v, v - tiles)

    @pl.loop(0, pairs.shape[1] // GROUP)
    def _(g):
        parts = []
        for j in range(GROUP):
            p = g * GROUP + j
            u, v = pairs[0, p], pairs[1, p]
            k = jnp.exp(dot(lefts[rows_of(u), :], rights[own_of(v)]) + SHIFT)
            k = jnp.where((p < count[0]) & (v < tiles), k, 0.0)
            parts.append((own_of(v), dot(k.T.astype(BF16), cotangent[rows_of(u), :])))
            u, v = pairs_below[0, p], pairs_below[1, p]
            k = jnp.exp(dot(lefts_below[rows_of(u), :], rights[own_of(v)]) + SHIFT)
            k = jnp.where((p < count_below[0]) & (v >= tiles), k, 0.0)
            parts.append((own_of(v), dot(k.T.astype(BF16), below[rows_of(u), :])))
        for t, part in parts:
            back[rows_of(t), :] += part

    mixed[...] = dot(back[...].astype(BF16), weight[...], ((1,), (1,)))


def near_ahead(seat, pairs, count, embedding, far, close, places, weight):
    atoms, channels = embedding.shape
    tiles = atoms // TILE
    hbm = pl.BlockSpec(memory_space=pltpu.HBM)
    return pl.pallas_call(
        ahead_kernel,
        out_shape=jax.ShapeDtypeStruct((atoms, channels), F32),
        in_specs=[SMEM] * 3 + [VMEM, hbm, hbm, VMEM, VMEM],
        out_specs=VMEM,
        scratch_shapes=[
            pltpu.VMEM((ROWS, channels), BF16),
            pltpu.VMEM((2 * atoms, channels), BF16),
            pltpu.VMEM((atoms, 96), BF16),
            pltpu.VMEM((2 * tiles, 96, TILE), BF16),
            pltpu.VMEM((3, atoms), F32),
            pltpu.SemaphoreType.DMA(()),
        ],
        compiler_params=pltpu.CompilerParams(vmem_limit_bytes=12 << 20),
        cost_estimate=pl.CostEstimate(flops=5 << 30, bytes_accessed=2 << 20, transcendentals=0),
        name="near_ahead",
    )(seat, pairs, count, embedding, in_hbm(far), in_hbm(close), places, weight)


def near_behind(seat, pairs, count, pairs_below, count_below, cotangent, far, close, places, weight):
    atoms, channels = cotangent.shape
    tiles = atoms // TILE
    hbm = pl.BlockSpec(memory_space=pltpu.HBM)
    return pl.pallas_call(
        behind_kernel,
        out_shape=jax.ShapeDtypeStruct((atoms, channels), F32),
        in_specs=[SMEM] * 5 + [VMEM, hbm, hbm, VMEM, VMEM],
        out_specs=VMEM,
        scratch_shapes=[
            pltpu.VMEM((ROWS, channels), BF16),
            pltpu.VMEM((atoms, channels), F32),
            pltpu.VMEM((atoms, 96), BF16),
            pltpu.VMEM((atoms, 96), BF16),
            pltpu.VMEM((tiles, 96, TILE), BF16),
            pltpu.VMEM((3, atoms), F32),
            pltpu.SemaphoreType.DMA(()),
        ],
        compiler_params=pltpu.CompilerParams(vmem_limit_bytes=12 << 20),
        cost_estimate=pl.CostEstimate(flops=5 << 30, bytes_accessed=2 << 20, transcendentals=0),
        name="near_behind",
    )(seat, pairs, count, pairs_below, count_below, cotangent, in_hbm(far), in_hbm(close), places, weight)


def final_kernel(seat, own, other, table, ahead, mixed, message, grad, matrix):
    channels = message.shape[1]

    @pl.when(pl.program_id(0) == 0)
    def _():
        for half, ref in ((seat[0], own), (1 - seat[0], other)):
            for r in range(0, 64, 2):
                rows = pl.ds(pl.multiple_of(half * 512 + 8 * r, 16), 16)
                for q in range(4):
                    pair = [ref[(r + d) * 4 + q].astype(F32) for d in range(2)]
                    matrix[rows, 128 * q : 128 * q + 128] = jnp.concatenate(pair, axis=0).astype(BF16)

    message[...] = (dot(table[...], matrix[:, :channels]) + ahead[...]).astype(BF16)
    grad[...] = (dot(table[...], matrix[:, channels:]) + mixed[...]).astype(BF16)


def final(seat, own, other, table, ahead, mixed, steps=2):
    atoms, channels = ahead.shape
    rows = atoms // steps
    block = pl.BlockSpec((rows, channels), lambda i: (i, 0))
    whole = pl.BlockSpec(own.shape, lambda i: (0, 0, 0), pipeline_mode=pl.Buffered(1))
    return pl.pallas_call(
        final_kernel,
        grid=(steps,),
        out_shape=(jax.ShapeDtypeStruct((atoms, channels), BF16),) * 2,
        in_specs=[
            SMEM,
            whole,
            whole,
            pl.BlockSpec((rows, table.shape[1]), lambda i: (i, 0)),
            block,
            block,
        ],
        out_specs=(block, block),
        scratch_shapes=[pltpu.VMEM((table.shape[1], 2 * channels), BF16)],
        compiler_params=pltpu.CompilerParams(vmem_limit_bytes=16 << 20),
        cost_estimate=pl.CostEstimate(flops=1 << 30, bytes_accessed=4 << 20, transcendentals=0),
        name="final",
    )(seat, own, other, *map(in_hbm, (table, ahead, mixed)))


def body(
    embedding, cotangent, fractional, wave_index, tile_pairs, counts, wave_filter, short_weight
):
    devices = math.prod(lax.axis_size(name) for name in FINE)
    atoms_all = embedding.shape[0] * devices
    core, x, y = (lax.axis_index(name).astype(jnp.int32) for name in ("core", "x", "y"))
    z_lo, z_hi = lax.axis_index("z_lo").astype(jnp.int32), lax.axis_index("z_hi").astype(jnp.int32)
    seat = jnp.stack([core, core * 32 + (y & 1) * 16 + x * 4 + z_lo, z_hi & 1])
    swap = [(0, 1), (1, 0)]

    listed = tile_pairs.T
    to_far, to_close = pack(seat[:1], embedding, cotangent, fractional, listed, counts)
    size = math.prod(lax.axis_size(name) for name in FINE)
    far = lax.ppermute(to_far, FINE, [(i, (i + (1 if i % 2 else -1)) % size) for i in range(size)])
    given = partial_sums(1 - seat[:1], wave_index, fractional, embedding, cotangent, True)
    given = lax.ppermute(given, "core", swap)
    kept = partial_sums(seat[:1], wave_index, fractional, embedding, cotangent, False)
    total = add(kept, given)
    chip = lax.all_to_all(total, ("y", "x"), 0, 0, tiled=True)
    close = lax.ppermute(to_close, "core", swap)
    table, scale = tables(seat, wave_index, fractional, wave_filter, atoms_all)
    summed = gather_sum(chip)
    parts = lax.all_to_all(summed, ALONG_Z, 0, 0, tiled=True)
    tail = jnp.where(seat[0] == 0, far[PAIRS:ROWS, :TILE], close[PAIRS:ROWS, :TILE]).astype(jnp.int32)
    pairs_below, count_below = tail[0:2, : listed.shape[1]], tail[LIVE - PAIRS, 0:1]
    mine = lax.all_to_all(coefficients(parts, scale), ALONG_Z, 0, 0, tiled=True)
    ahead = near_ahead(seat[:1], listed, counts, embedding, far, close, fractional, short_weight)
    mixed = near_behind(
        seat[:1], listed, counts, pairs_below, count_below, cotangent, far, close, fractional, short_weight
    )
    coeffs = lax.all_to_all(copies(mine), ("y", "x"), 0, 0, tiled=True).reshape(256, 8, 128)
    other = lax.ppermute(coeffs, "core", swap)
    return final(seat, coeffs, other, table, ahead, mixed)


def solution(mesh):
    fine = Mesh(mesh.devices.reshape(4, 4, 4, 4, 2), FINE)
    rows, places, one = P(FINE, None), P(None, FINE), P(FINE)
    return jax.shard_map(
        body,
        mesh=fine,
        in_specs=(rows, rows, places, P(), rows, one, P(), P()),
        out_specs=(rows, rows),
        check_vma=False,
    )
```

```python
import functools
import math

import jax
import jax.numpy as jnp
from jax import lax
from jax.experimental import pallas as pl
from jax.experimental.pallas import tpu as pltpu
from jax.sharding import Mesh
from jax.sharding import PartitionSpec as P


TILE = 128
FINE = ("z_lo", "y", "x", "z_hi", "core")
ALONG_Z = ("z_lo", "z_hi")
F32, BF16 = jnp.float32, jnp.bfloat16
VMEM = pl.BlockSpec(memory_space=pltpu.VMEM)
SMEM = pl.BlockSpec(memory_space=pltpu.SMEM)

COS = (
    0.9999999889445764,
    -19.73920446657614,
    64.93911592834654,
    -85.45011342750612,
    60.167429791960785,
    -25.966884612677454,
    6.527705963152031,
)
SIN = (
    6.283185302468581,
    -41.34170039298386,
    81.60513081114435,
    -76.70300555818746,
    42.02585148963868,
    -14.899578436725896,
    3.2377800860428168,
)


def cos_sin(turns):
    r = turns - jnp.floor(turns + 0.5)
    u = r * r
    c, s = COS[-1], SIN[-1]
    for k in COS[-2::-1]:
        c = c * u + k
    for k in SIN[-2::-1]:
        s = s * u + k
    return c, s * r


def dot(a, b, dims=((1,), (0,))):
    return lax.dot_general(a, b, (dims, ((), ())), preferred_element_type=F32)


def padded(rows):
    rows = rows.astype(F32)
    return jnp.concatenate([rows, jnp.zeros((5, rows.shape[1]), F32)], axis=0)


def sums_kernel(seat, waves_far, places_far, left_far, right_far, out, waves, places, left, right, turns, table, sems):
    half, atoms = turns.shape
    mine = pl.ds(pl.multiple_of(seat[0] * half, half), half)
    loads = [
        pltpu.make_async_copy(waves_far.at[:, mine], waves, sems.at[0]),
        pltpu.make_async_copy(places_far, places, sems.at[1]),
        pltpu.make_async_copy(left_far, left, sems.at[2]),
        pltpu.make_async_copy(right_far, right, sems.at[3]),
    ]
    for load in loads:
        load.start()
    loads[0].wait()
    loads[1].wait()
    turns[...] = dot(padded(waves[...]).astype(BF16), padded(places[...]).astype(BF16), ((0,), (0,)))

    @pl.loop(0, half // 16)
    def _(i):
        top = pl.ds(pl.multiple_of(i * 16, 16), 16)
        low = pl.ds(pl.multiple_of(half + i * 16, 16), 16)
        for j in range(atoms // 256):
            cols = pl.ds(j * 256, 256)
            c, s = cos_sin(turns[top, cols])
            table[top, cols] = c.astype(BF16)
            table[low, cols] = s.astype(BF16)

    for side, ref in enumerate((left, right)):
        loads[2 + side].wait()
        for block in range(2):
            part = dot(table[block * half : block * half + half, :], ref[...])
            for r in range(half // 8):
                i, k = divmod(block * (half // 8) + r, 4)
                for q in range(2):
                    out[i, k * 4 + side * 2 + q] = part[8 * r : 8 * r + 8, 128 * q : 128 * q + 128]


def partial_sums(seat, waves, places, left, right, first):
    half, atoms = waves.shape[1] // 2, places.shape[1]
    return pl.pallas_call(
        sums_kernel,
        out_shape=jax.ShapeDtypeStruct((16, 16, 8, 128), F32),
        in_specs=[SMEM] + [pl.BlockSpec(memory_space=pl.ANY)] * 4,
        out_specs=VMEM,
        scratch_shapes=[
            pltpu.VMEM((3, half), waves.dtype),
            pltpu.VMEM(places.shape, BF16),
            pltpu.VMEM(left.shape, BF16),
            pltpu.VMEM(right.shape, BF16),
            pltpu.VMEM((half, atoms), F32),
            pltpu.VMEM((2 * half, atoms), BF16),
            pltpu.SemaphoreType.DMA((4,)),
        ],
        compiler_params=pltpu.CompilerParams(vmem_limit_bytes=12 << 20),
        cost_estimate=pl.CostEstimate(
            flops=4 * half * atoms * 512, bytes_accessed=2 << 20, transcendentals=0
        ),
        name="sums",
    )(seat, *(map(in_hbm, (waves, places)) if first else (waves, places)), in_hbm(left), in_hbm(right))


def add_kernel(a, b, out):
    @pl.loop(0, a.shape[0])
    def _(i):
        out[i] = (a[i] + b[i]).astype(BF16)


def add(a, b):
    return pl.pallas_call(
        add_kernel,
        out_shape=jax.ShapeDtypeStruct(a.shape, BF16),
        in_specs=[VMEM] * 2,
        out_specs=VMEM,
        compiler_params=pltpu.CompilerParams(vmem_limit_bytes=4 << 20),
        name="add",
    )(a, b)


def gather_sum_kernel(a, out):
    @pl.loop(0, out.shape[0])
    def _(i):
        total = a[0, i].astype(F32)
        for k in range(1, a.shape[0]):
            total = total + a[k, i].astype(F32)
        out[i] = total


def gather_sum(a):
    return pl.pallas_call(
        gather_sum_kernel,
        out_shape=jax.ShapeDtypeStruct(a.shape[1:], F32),
        in_specs=[VMEM],
        out_specs=VMEM,
        compiler_params=pltpu.CompilerParams(vmem_limit_bytes=4 << 20),
        name="plane_sum",
    )(a)


def coefficients_kernel(a, scale, out):
    total = a[0]
    for k in range(1, a.shape[0]):
        total = total + a[k]
    mine = (total * scale[...]).astype(BF16)
    for k in range(out.shape[0]):
        out[k] = mine


def coefficients(a, scale):
    return pl.pallas_call(
        coefficients_kernel,
        out_shape=jax.ShapeDtypeStruct(a.shape, BF16),
        in_specs=[VMEM] * 2,
        out_specs=VMEM,
        compiler_params=pltpu.CompilerParams(vmem_limit_bytes=4 << 20),
        name="coefficients",
    )(a, scale)


def copies_kernel(a, out):
    for k in range(a.shape[0]):
        mine = a[k]

        @pl.loop(0, out.shape[0], unroll=True)
        def _(i):
            out[i, k] = mine


def copies(a):
    return pl.pallas_call(
        copies_kernel,
        out_shape=jax.ShapeDtypeStruct((16, *a.shape), BF16),
        in_specs=[VMEM],
        out_specs=VMEM,
        compiler_params=pltpu.CompilerParams(vmem_limit_bytes=4 << 20),
        name="copies",
    )(a)


def table_kernel(waves, places, table, turns):
    atoms, count = turns.shape
    half = count // 2
    turns[...] = dot(padded(places[...]).astype(BF16), padded(waves[...]).astype(BF16), ((0,), (0,)))

    @pl.loop(0, atoms // 16)
    def _(i):
        rows = pl.ds(pl.multiple_of(i * 16, 16), 16)
        for j in range(2):
            c, s = cos_sin(turns[rows, j * half : j * half + half])
            table[rows, 2 * j * half : (2 * j + 1) * half] = c.astype(BF16)
            table[rows, (2 * j + 1) * half : (2 * j + 2) * half] = s.astype(BF16)


def tables(waves, places):
    atoms, count = places.shape[1], waves.shape[1]
    return pl.pallas_call(
        table_kernel,
        out_shape=jax.ShapeDtypeStruct((atoms, 2 * count), BF16),
        in_specs=[VMEM] * 2,
        out_specs=VMEM,
        scratch_shapes=[pltpu.VMEM((atoms, count), F32)],
        compiler_params=pltpu.CompilerParams(vmem_limit_bytes=8 << 20),
        cost_estimate=pl.CostEstimate(flops=6 << 30, bytes_accessed=2 << 20, transcendentals=0),
        name="table",
    )(waves, places)


def thirds(value):
    a = value.astype(BF16).astype(F32)
    b = (value - a).astype(BF16).astype(F32)
    return a, b, value - a - b


def features(places):
    coords = padded(places)
    live = lax.broadcasted_iota(jnp.int32, coords.shape, 0) < 3
    parts = [thirds(jnp.where(live, v, 0.0)) for v in cos_sin(coords)]
    left = jnp.concatenate([p[k] for k in (0, 0, 1, 1, 0, 2) for p in parts], axis=0)
    right = jnp.concatenate([p[k] for k in (0, 1, 0, 1, 2, 0) for p in parts], axis=0)
    return left, right


PLACES, PAIRS, LIVE, ROWS = 1024, 1040, 1048, 1056


def pack_kernel(seat, embedding, cotangent, places_far, pairs_far, count, far, close, places, pairs, sems):
    atoms = embedding.shape[0]
    small = [
        pltpu.make_async_copy(places_far, places, sems.at[2]),
        pltpu.make_async_copy(pairs_far, pairs, sems.at[3]),
    ]
    for load in small:
        load.start()

    def both(forward, backward):
        a = pltpu.make_async_copy(embedding, backward.at[pl.ds(0, atoms)], sems.at[0])
        b = pltpu.make_async_copy(cotangent, forward.at[pl.ds(0, atoms)], sems.at[1])
        a.start()
        b.start()
        return a, b

    @pl.when(seat[0] == 0)
    def _():
        both(close, far)

    @pl.when(seat[0] != 0)
    def _():
        both(far, close)

    width = far.shape[1]
    for load in small:
        load.wait()
    coords = places[...].astype(F32)
    rows = [coords[d : d + 1, k * width : k * width + width] for d in range(3) for k in range(4)]
    rows = jnp.concatenate([*rows, jnp.zeros((4, width), F32)], axis=0).astype(BF16)
    listed = jnp.concatenate([pairs[...].astype(F32), jnp.zeros((2, width - pairs.shape[1]), F32)], axis=1)
    listed = jnp.concatenate([listed, jnp.zeros((6, width), F32)], axis=0)
    tail = jnp.concatenate([listed, jnp.full((8, width), count[0], jnp.int32).astype(F32)], axis=0).astype(BF16)
    for ref in (far, close):
        ref[PLACES:PAIRS, :] = rows
        ref[PAIRS:ROWS, :] = tail
    pltpu.make_async_copy(embedding, far.at[pl.ds(0, atoms)], sems.at[0]).wait()
    pltpu.make_async_copy(cotangent, close.at[pl.ds(0, atoms)], sems.at[1]).wait()


def pack(seat, embedding, cotangent, places, pairs, count):
    hbm = pl.BlockSpec(memory_space=pltpu.HBM)
    return pl.pallas_call(
        pack_kernel,
        out_shape=(jax.ShapeDtypeStruct((ROWS, embedding.shape[1]), BF16),) * 2,
        in_specs=[SMEM, hbm, hbm, hbm, hbm, SMEM],
        out_specs=(VMEM, VMEM),
        scratch_shapes=[
            pltpu.VMEM(places.shape, BF16),
            pltpu.VMEM(pairs.shape, pairs.dtype),
            pltpu.SemaphoreType.DMA((4,)),
        ],
        compiler_params=pltpu.CompilerParams(vmem_limit_bytes=4 << 20),
        name="pack",
    )(seat, *map(in_hbm, (embedding, cotangent, places, pairs)), count)


def in_hbm(value):
    return pltpu.with_memory_space_constraint(value, pltpu.HBM)


GROUP = 4
SHIFT = -3.0 - 0.5 * math.log(TILE)


def rows_of(t):
    return pl.ds(pl.multiple_of(t * TILE, TILE), TILE)


def unpack_places(packed, places):
    width = packed.shape[1]
    rows = packed[PLACES:PAIRS, :].astype(F32)
    for d in range(3):
        for k in range(4):
            places[d : d + 1, k * width : k * width + width] = rows[4 * d + k : 4 * d + k + 1]


def store_tiles(rights, first, right):
    for t in range(right.shape[1] // TILE):
        rights[first + t] = right[:, t * TILE : t * TILE + TILE].astype(BF16)


def ahead_kernel(
    seat, pairs, count, embedding, far, close, places, weight, wave_filter,
    ahead, scale,
    above, projected, lefts, rights, far_places, tile, sem, tile_sem, *, atoms_all,
):
    atoms = embedding.shape[0]
    mine = wave_filter.at[
        pl.ds(pl.multiple_of(seat[1] * 8, 8), 8), pl.ds(pl.multiple_of(seat[2] * TILE, TILE), TILE)
    ]
    filtering = pltpu.make_async_copy(mine, tile, tile_sem)
    filtering.start()

    @pl.when(seat[0] == 0)
    def _():
        pltpu.make_async_copy(close, above, sem).start()

    @pl.when(seat[0] != 0)
    def _():
        pltpu.make_async_copy(far, above, sem).start()

    projected[pl.ds(0, atoms), :] = dot(embedding[...], weight[...]).astype(BF16)
    left, right = features(places[...])
    lefts[...] = left.T.astype(BF16)
    store_tiles(rights, 0, right)
    ahead[...] = jnp.zeros_like(ahead)
    filtering.wait()
    scale[...] = tile[...] * (1.0 / math.sqrt(atoms_all))
    pltpu.make_async_copy(far, above, sem).wait()
    projected[pl.ds(atoms, atoms), :] = dot(above[pl.ds(0, atoms), :], weight[...]).astype(BF16)
    unpack_places(above, far_places)
    _, right = features(far_places[...])
    store_tiles(rights, atoms // TILE, right)

    @pl.loop(0, pairs.shape[1] // GROUP)
    def _(g):
        parts = []
        for j in range(GROUP):
            p = g * GROUP + j
            u, v = pairs[0, p], pairs[1, p]
            k = jnp.exp(dot(lefts[rows_of(u), :], rights[v]) + SHIFT)
            k = jnp.where(p < count[0], k, 0.0).astype(BF16)
            parts.append((u, dot(k, projected[rows_of(v), :])))
        for t, part in parts:
            ahead[rows_of(t), :] += part


def behind_kernel(
    seat, pairs, count, pairs_below, count_below, cotangent, far, close, places, weight,
    mixed,
    sources, back, lefts, rights, far_places, listed, sem, own_sem,
):
    atoms = cotangent.shape[0]
    tiles = atoms // TILE
    own = pltpu.make_async_copy(cotangent, sources.at[pl.ds(0, atoms)], own_sem)
    own.start()
    packed = sources.at[pl.ds(atoms, ROWS)]

    @pl.when(seat[0] == 0)
    def _():
        pltpu.make_async_copy(far, packed, sem).start()

    @pl.when(seat[0] != 0)
    def _():
        pltpu.make_async_copy(close, packed, sem).start()

    live = jnp.int32(0)
    for p in range(pairs.shape[1]):
        u, v = pairs[0, p], pairs[1, p]
        listed[0, live] = u
        listed[1, live] = jnp.where(v < tiles, v, v - tiles)
        live = live + jnp.where((p < count[0]) & (v < tiles), 1, 0)
        u, v = pairs_below[0, p], pairs_below[1, p]
        listed[0, live] = u + tiles
        listed[1, live] = jnp.where(v < tiles, v, v - tiles)
        live = live + jnp.where((p < count_below[0]) & (v >= tiles), 1, 0)
    for j in range(GROUP):
        listed[0, live + j] = jnp.int32(0)
        listed[1, live + j] = jnp.int32(0)

    left, right = features(places[...])
    lefts[pl.ds(0, atoms), :] = left.T.astype(BF16)
    store_tiles(rights, 0, right)
    back[...] = jnp.zeros_like(back)
    own.wait()
    pltpu.make_async_copy(far, packed, sem).wait()
    unpack_places(packed, far_places)
    left, _ = features(far_places[...])
    lefts[pl.ds(atoms, atoms), :] = left.T.astype(BF16)

    @pl.loop(0, lax.shift_right_logical(live + (GROUP - 1), 2))
    def _(g):
        parts = []
        for j in range(GROUP):
            p = g * GROUP + j
            u, v = listed[0, p], listed[1, p]
            k = jnp.exp(dot(lefts[rows_of(u), :], rights[v]) + SHIFT)
            k = jnp.where(p < live, k, 0.0)
            parts.append((v, dot(k.T.astype(BF16), sources[rows_of(u), :])))
        for t, part in parts:
            back[rows_of(t), :] += part

    mixed[...] = dot(back[...].astype(BF16), weight[...], ((1,), (1,)))


def near_ahead(seat, pairs, count, embedding, far, close, places, weight, wave_filter, atoms_all):
    atoms, channels = embedding.shape
    tiles = atoms // TILE
    hbm = pl.BlockSpec(memory_space=pltpu.HBM)
    return pl.pallas_call(
        functools.partial(ahead_kernel, atoms_all=atoms_all),
        out_shape=(
            jax.ShapeDtypeStruct((atoms, channels), F32),
            jax.ShapeDtypeStruct((8, TILE), F32),
        ),
        in_specs=[SMEM] * 3 + [VMEM, hbm, hbm, VMEM, VMEM, hbm],
        out_specs=(VMEM, VMEM),
        scratch_shapes=[
            pltpu.VMEM((ROWS, channels), BF16),
            pltpu.VMEM((2 * atoms, channels), BF16),
            pltpu.VMEM((atoms, 96), BF16),
            pltpu.VMEM((2 * tiles, 96, TILE), BF16),
            pltpu.VMEM((3, atoms), F32),
            pltpu.VMEM((8, TILE), F32),
            pltpu.SemaphoreType.DMA(()),
            pltpu.SemaphoreType.DMA(()),
        ],
        compiler_params=pltpu.CompilerParams(vmem_limit_bytes=12 << 20),
        cost_estimate=pl.CostEstimate(flops=5 << 30, bytes_accessed=2 << 20, transcendentals=0),
        name="near_ahead",
    )(seat, pairs, count, embedding, in_hbm(far), in_hbm(close), places, weight, in_hbm(wave_filter))


def near_behind(seat, pairs, count, pairs_below, count_below, cotangent, far, close, places, weight):
    atoms, channels = cotangent.shape
    tiles = atoms // TILE
    hbm = pl.BlockSpec(memory_space=pltpu.HBM)
    return pl.pallas_call(
        behind_kernel,
        out_shape=jax.ShapeDtypeStruct((atoms, channels), F32),
        in_specs=[SMEM] * 5 + [hbm] * 3 + [VMEM, VMEM],
        out_specs=VMEM,
        scratch_shapes=[
            pltpu.VMEM((atoms + ROWS, channels), BF16),
            pltpu.VMEM((atoms, channels), F32),
            pltpu.VMEM((2 * atoms, 96), BF16),
            pltpu.VMEM((tiles, 96, TILE), BF16),
            pltpu.VMEM((3, atoms), F32),
            pltpu.SMEM((2, 2 * pairs.shape[1] + GROUP), jnp.int32),
            pltpu.SemaphoreType.DMA(()),
            pltpu.SemaphoreType.DMA(()),
        ],
        compiler_params=pltpu.CompilerParams(vmem_limit_bytes=12 << 20),
        cost_estimate=pl.CostEstimate(flops=5 << 30, bytes_accessed=2 << 20, transcendentals=0),
        name="near_behind",
    )(
        seat, pairs, count, pairs_below, count_below, in_hbm(cotangent), in_hbm(far), in_hbm(close), places, weight
    )


def final_kernel(seat, own, other, table, ahead, mixed, message, grad, matrix):
    channels = message.shape[1]

    @pl.when(pl.program_id(0) == 0)
    def _():
        for half, ref in ((seat[0], own), (1 - seat[0], other)):
            for r in range(0, 64, 2):
                rows = pl.ds(pl.multiple_of(half * 512 + 8 * r, 16), 16)
                for q in range(4):
                    pair = [ref[(r + d) * 4 + q].astype(F32) for d in range(2)]
                    matrix[rows, 128 * q : 128 * q + 128] = jnp.concatenate(pair, axis=0).astype(BF16)

    message[...] = (dot(table[...], matrix[:, :channels]) + ahead[...]).astype(BF16)
    grad[...] = (dot(table[...], matrix[:, channels:]) + mixed[...]).astype(BF16)


def final(seat, own, other, table, ahead, mixed, steps=2):
    atoms, channels = ahead.shape
    rows = atoms // steps
    block = pl.BlockSpec((rows, channels), lambda i: (i, 0))
    whole = pl.BlockSpec(own.shape, lambda i: (0, 0, 0), pipeline_mode=pl.Buffered(1))
    return pl.pallas_call(
        final_kernel,
        grid=(steps,),
        out_shape=(jax.ShapeDtypeStruct((atoms, channels), BF16),) * 2,
        in_specs=[
            SMEM,
            whole,
            whole,
            pl.BlockSpec((rows, table.shape[1]), lambda i: (i, 0)),
            block,
            block,
        ],
        out_specs=(block, block),
        scratch_shapes=[pltpu.VMEM((table.shape[1], 2 * channels), BF16)],
        compiler_params=pltpu.CompilerParams(vmem_limit_bytes=16 << 20),
        cost_estimate=pl.CostEstimate(flops=1 << 30, bytes_accessed=4 << 20, transcendentals=0),
        name="final",
    )(seat, own, other, table, in_hbm(ahead), in_hbm(mixed))


def body(
    embedding, cotangent, fractional, wave_index, tile_pairs, counts, wave_filter, short_weight
):
    devices = math.prod(lax.axis_size(name) for name in FINE)
    atoms_all = embedding.shape[0] * devices
    core, x, y = (lax.axis_index(name).astype(jnp.int32) for name in ("core", "x", "y"))
    z_lo, z_hi = lax.axis_index("z_lo").astype(jnp.int32), lax.axis_index("z_hi").astype(jnp.int32)
    seat = jnp.stack([core, core * 32 + (y & 1) * 16 + x * 4 + z_lo, z_hi & 1])
    swap = [(0, 1), (1, 0)]

    listed = tile_pairs.T
    to_far, to_close = pack(seat[:1], embedding, cotangent, fractional, listed, counts)
    size = math.prod(lax.axis_size(name) for name in FINE)
    far = lax.ppermute(to_far, FINE, [(i, (i + (1 if i % 2 else -1)) % size) for i in range(size)])
    given = partial_sums(1 - seat[:1], wave_index, fractional, embedding, cotangent, True)
    given = lax.ppermute(given, "core", swap)
    kept = partial_sums(seat[:1], wave_index, fractional, embedding, cotangent, False)
    total = add(kept, given)
    chip = lax.all_to_all(total, ("y", "x"), 0, 0, tiled=True)
    close = lax.ppermute(to_close, "core", swap)
    table = tables(wave_index, fractional)
    summed = gather_sum(chip)
    parts = lax.all_to_all(summed, ALONG_Z, 0, 0, tiled=True)
    tail = jnp.where(seat[0] == 0, far[PAIRS:ROWS, :TILE], close[PAIRS:ROWS, :TILE]).astype(jnp.int32)
    pairs_below, count_below = tail[0:2, : listed.shape[1]], tail[LIVE - PAIRS, 0:1]
    ahead, scale = near_ahead(
        seat, listed, counts, embedding, far, close, fractional, short_weight, wave_filter, atoms_all
    )
    mine = lax.all_to_all(coefficients(parts, scale), ALONG_Z, 0, 0, tiled=True)
    mixed = near_behind(
        seat[:1], listed, counts, pairs_below, count_below, cotangent, far, close, fractional, short_weight
    )
    coeffs = lax.all_to_all(copies(mine), ("y", "x"), 0, 0, tiled=True).reshape(256, 8, 128)
    other = lax.ppermute(coeffs, "core", swap)
    return final(seat, coeffs, other, table, ahead, mixed)


def solution(mesh):
    fine = Mesh(mesh.devices.reshape(4, 4, 4, 4, 2), FINE)
    rows, places, one = P(FINE, None), P(None, FINE), P(FINE)
    return jax.shard_map(
        body,
        mesh=fine,
        in_specs=(rows, rows, places, P(), rows, one, P(), P()),
        out_specs=(rows, rows),
        check_vma=False,
    )
```

```python
import functools
import math

import jax
import jax.numpy as jnp
from jax import lax
from jax.experimental import pallas as pl
from jax.experimental.pallas import tpu as pltpu
from jax.sharding import Mesh
from jax.sharding import PartitionSpec as P


TILE = 128
FINE = ("z_lo", "y", "x", "z_hi", "core")
ALONG_Z = ("z_lo", "z_hi")
F32, BF16 = jnp.float32, jnp.bfloat16
VMEM = pl.BlockSpec(memory_space=pltpu.VMEM)
SMEM = pl.BlockSpec(memory_space=pltpu.SMEM)

COS = (
    0.9999999889445764,
    -19.73920446657614,
    64.93911592834654,
    -85.45011342750612,
    60.167429791960785,
    -25.966884612677454,
    6.527705963152031,
)
SIN = (
    6.283185302468581,
    -41.34170039298386,
    81.60513081114435,
    -76.70300555818746,
    42.02585148963868,
    -14.899578436725896,
    3.2377800860428168,
)


def cos_sin(turns):
    r = turns - jnp.floor(turns + 0.5)
    u = r * r
    c, s = COS[-1], SIN[-1]
    for k in COS[-2::-1]:
        c = c * u + k
    for k in SIN[-2::-1]:
        s = s * u + k
    return c, s * r


def dot(a, b, dims=((1,), (0,))):
    return lax.dot_general(a, b, (dims, ((), ())), preferred_element_type=F32)


def padded(rows):
    rows = rows.astype(F32)
    return jnp.concatenate([rows, jnp.zeros((5, rows.shape[1]), F32)], axis=0)


def sums_kernel(seat, waves_far, places_far, left_far, right_far, out, waves, places, left, right, turns, table, sems):
    half, atoms = turns.shape
    mine = pl.ds(pl.multiple_of(seat[0] * half, half), half)
    loads = [
        pltpu.make_async_copy(waves_far.at[:, mine], waves, sems.at[0]),
        pltpu.make_async_copy(places_far, places, sems.at[1]),
        pltpu.make_async_copy(left_far, left, sems.at[2]),
        pltpu.make_async_copy(right_far, right, sems.at[3]),
    ]
    for load in loads:
        load.start()
    loads[0].wait()
    loads[1].wait()
    turns[...] = dot(padded(waves[...]).astype(BF16), padded(places[...]).astype(BF16), ((0,), (0,)))

    @pl.loop(0, half // 16)
    def _(i):
        top = pl.ds(pl.multiple_of(i * 16, 16), 16)
        low = pl.ds(pl.multiple_of(half + i * 16, 16), 16)
        for j in range(atoms // 256):
            cols = pl.ds(j * 256, 256)
            c, s = cos_sin(turns[top, cols])
            table[top, cols] = c.astype(BF16)
            table[low, cols] = s.astype(BF16)

    for side, ref in enumerate((left, right)):
        loads[2 + side].wait()
        for block in range(2):
            part = dot(table[block * half : block * half + half, :], ref[...])
            for r in range(half // 8):
                i, k = divmod(block * (half // 8) + r, 4)
                for q in range(2):
                    out[i, k * 4 + side * 2 + q] = part[8 * r : 8 * r + 8, 128 * q : 128 * q + 128]


def partial_sums(seat, waves, places, left, right, first):
    half, atoms = waves.shape[1] // 2, places.shape[1]
    return pl.pallas_call(
        sums_kernel,
        out_shape=jax.ShapeDtypeStruct((16, 16, 8, 128), F32),
        in_specs=[SMEM] + [pl.BlockSpec(memory_space=pl.ANY)] * 4,
        out_specs=VMEM,
        scratch_shapes=[
            pltpu.VMEM((3, half), waves.dtype),
            pltpu.VMEM(places.shape, BF16),
            pltpu.VMEM(left.shape, BF16),
            pltpu.VMEM(right.shape, BF16),
            pltpu.VMEM((half, atoms), F32),
            pltpu.VMEM((2 * half, atoms), BF16),
            pltpu.SemaphoreType.DMA((4,)),
        ],
        compiler_params=pltpu.CompilerParams(vmem_limit_bytes=12 << 20),
        cost_estimate=pl.CostEstimate(
            flops=4 * half * atoms * 512, bytes_accessed=2 << 20, transcendentals=0
        ),
        name="sums",
    )(seat, *(map(in_hbm, (waves, places)) if first else (waves, places)), in_hbm(left), in_hbm(right))


def add_kernel(a, b, out):
    @pl.loop(0, a.shape[0])
    def _(i):
        out[i] = (a[i] + b[i]).astype(BF16)


def add(a, b):
    return pl.pallas_call(
        add_kernel,
        out_shape=jax.ShapeDtypeStruct(a.shape, BF16),
        in_specs=[VMEM] * 2,
        out_specs=VMEM,
        compiler_params=pltpu.CompilerParams(vmem_limit_bytes=4 << 20),
        name="add",
    )(a, b)


def gather_sum_kernel(a, out):
    @pl.loop(0, out.shape[0])
    def _(i):
        total = a[0, i].astype(F32)
        for k in range(1, a.shape[0]):
            total = total + a[k, i].astype(F32)
        out[i] = total


def gather_sum(a):
    return pl.pallas_call(
        gather_sum_kernel,
        out_shape=jax.ShapeDtypeStruct(a.shape[1:], F32),
        in_specs=[VMEM],
        out_specs=VMEM,
        compiler_params=pltpu.CompilerParams(vmem_limit_bytes=4 << 20),
        name="plane_sum",
    )(a)


def coefficients_kernel(a, scale, out):
    total = a[0]
    for k in range(1, a.shape[0]):
        total = total + a[k]
    mine = (total * scale[...]).astype(BF16)
    for k in range(out.shape[0]):
        out[k] = mine


def coefficients(a, scale):
    return pl.pallas_call(
        coefficients_kernel,
        out_shape=jax.ShapeDtypeStruct(a.shape, BF16),
        in_specs=[VMEM] * 2,
        out_specs=VMEM,
        compiler_params=pltpu.CompilerParams(vmem_limit_bytes=4 << 20),
        name="coefficients",
    )(a, scale)


def copies_kernel(a, out):
    for k in range(a.shape[0]):
        mine = a[k]

        @pl.loop(0, out.shape[0], unroll=True)
        def _(i):
            out[i, k] = mine


def copies(a):
    return pl.pallas_call(
        copies_kernel,
        out_shape=jax.ShapeDtypeStruct((16, *a.shape), BF16),
        in_specs=[VMEM],
        out_specs=VMEM,
        compiler_params=pltpu.CompilerParams(vmem_limit_bytes=4 << 20),
        name="copies",
    )(a)


def table_kernel(waves, places, table, turns):
    atoms, count = turns.shape
    half = count // 2
    turns[...] = dot(padded(places[...]).astype(BF16), padded(waves[...]).astype(BF16), ((0,), (0,)))

    @pl.loop(0, atoms // 16)
    def _(i):
        rows = pl.ds(pl.multiple_of(i * 16, 16), 16)
        for j in range(2):
            c, s = cos_sin(turns[rows, j * half : j * half + half])
            table[rows, 2 * j * half : (2 * j + 1) * half] = c.astype(BF16)
            table[rows, (2 * j + 1) * half : (2 * j + 2) * half] = s.astype(BF16)


def tables(waves, places):
    atoms, count = places.shape[1], waves.shape[1]
    return pl.pallas_call(
        table_kernel,
        out_shape=jax.ShapeDtypeStruct((atoms, 2 * count), BF16),
        in_specs=[VMEM] * 2,
        out_specs=VMEM,
        scratch_shapes=[pltpu.VMEM((atoms, count), F32)],
        compiler_params=pltpu.CompilerParams(vmem_limit_bytes=8 << 20),
        cost_estimate=pl.CostEstimate(flops=6 << 30, bytes_accessed=2 << 20, transcendentals=0),
        name="table",
    )(waves, places)


def thirds(value):
    a = value.astype(BF16).astype(F32)
    b = (value - a).astype(BF16).astype(F32)
    return a, b, value - a - b


def features(places):
    coords = padded(places)
    live = lax.broadcasted_iota(jnp.int32, coords.shape, 0) < 3
    parts = [thirds(jnp.where(live, v, 0.0)) for v in cos_sin(coords)]
    left = jnp.concatenate([p[k] for k in (0, 0, 1, 1, 0, 2) for p in parts], axis=0)
    right = jnp.concatenate([p[k] for k in (0, 1, 0, 1, 2, 0) for p in parts], axis=0)
    return left, right


PLACES, PAIRS, LIVE, ROWS = 1024, 1040, 1048, 1056


def pack_kernel(seat, embedding, cotangent, places_far, pairs_far, count, far, close, places, pairs, sems):
    atoms = embedding.shape[0]
    small = [
        pltpu.make_async_copy(places_far, places, sems.at[2]),
        pltpu.make_async_copy(pairs_far, pairs, sems.at[3]),
    ]
    for load in small:
        load.start()

    def both(forward, backward):
        a = pltpu.make_async_copy(embedding, backward.at[pl.ds(0, atoms)], sems.at[0])
        b = pltpu.make_async_copy(cotangent, forward.at[pl.ds(0, atoms)], sems.at[1])
        a.start()
        b.start()
        return a, b

    @pl.when(seat[0] == 0)
    def _():
        both(close, far)

    @pl.when(seat[0] != 0)
    def _():
        both(far, close)

    width = far.shape[1]
    for load in small:
        load.wait()
    coords = places[...].astype(F32)
    rows = [coords[d : d + 1, k * width : k * width + width] for d in range(3) for k in range(4)]
    rows = jnp.concatenate([*rows, jnp.zeros((4, width), F32)], axis=0).astype(BF16)
    listed = jnp.concatenate([pairs[...].astype(F32), jnp.zeros((2, width - pairs.shape[1]), F32)], axis=1)
    listed = jnp.concatenate([listed, jnp.zeros((6, width), F32)], axis=0)
    tail = jnp.concatenate([listed, jnp.full((8, width), count[0], jnp.int32).astype(F32)], axis=0).astype(BF16)
    for ref in (far, close):
        ref[PLACES:PAIRS, :] = rows
        ref[PAIRS:ROWS, :] = tail
    pltpu.make_async_copy(embedding, far.at[pl.ds(0, atoms)], sems.at[0]).wait()
    pltpu.make_async_copy(cotangent, close.at[pl.ds(0, atoms)], sems.at[1]).wait()


def pack(seat, embedding, cotangent, places, pairs, count):
    hbm = pl.BlockSpec(memory_space=pltpu.HBM)
    return pl.pallas_call(
        pack_kernel,
        out_shape=(jax.ShapeDtypeStruct((ROWS, embedding.shape[1]), BF16),) * 2,
        in_specs=[SMEM, hbm, hbm, hbm, hbm, SMEM],
        out_specs=(VMEM, VMEM),
        scratch_shapes=[
            pltpu.VMEM(places.shape, BF16),
            pltpu.VMEM(pairs.shape, pairs.dtype),
            pltpu.SemaphoreType.DMA((4,)),
        ],
        compiler_params=pltpu.CompilerParams(vmem_limit_bytes=4 << 20),
        name="pack",
    )(seat, *map(in_hbm, (embedding, cotangent, places, pairs)), count)


def in_hbm(value):
    return pltpu.with_memory_space_constraint(value, pltpu.HBM)


GROUP = 4
SHIFT = -3.0 - 0.5 * math.log(TILE)


def rows_of(t):
    return pl.ds(pl.multiple_of(t * TILE, TILE), TILE)


def unpack_places(packed, places):
    width = packed.shape[1]
    rows = packed[PLACES:PAIRS, :].astype(F32)
    for d in range(3):
        for k in range(4):
            places[d : d + 1, k * width : k * width + width] = rows[4 * d + k : 4 * d + k + 1]


def store_tiles(rights, first, right):
    for t in range(right.shape[1] // TILE):
        rights[first + t] = right[:, t * TILE : t * TILE + TILE].astype(BF16)


def ahead_kernel(
    seat, pairs, count, embedding, far, close, places, weight, wave_filter,
    ahead, scale,
    above, projected, lefts, rights, far_places, tile, sem, tile_sem, *, atoms_all,
):
    atoms = embedding.shape[0]
    mine = wave_filter.at[
        pl.ds(pl.multiple_of(seat[1] * 8, 8), 8), pl.ds(pl.multiple_of(seat[2] * TILE, TILE), TILE)
    ]
    filtering = pltpu.make_async_copy(mine, tile, tile_sem)
    filtering.start()

    @pl.when(seat[0] == 0)
    def _():
        pltpu.make_async_copy(close, above, sem).start()

    @pl.when(seat[0] != 0)
    def _():
        pltpu.make_async_copy(far, above, sem).start()

    projected[pl.ds(0, atoms), :] = dot(embedding[...], weight[...]).astype(BF16)
    left, right = features(places[...])
    lefts[...] = left.T.astype(BF16)
    store_tiles(rights, 0, right)
    ahead[...] = jnp.zeros_like(ahead)
    filtering.wait()
    scale[...] = tile[...] * (1.0 / math.sqrt(atoms_all))
    pltpu.make_async_copy(far, above, sem).wait()
    projected[pl.ds(atoms, atoms), :] = dot(above[pl.ds(0, atoms), :], weight[...]).astype(BF16)
    unpack_places(above, far_places)
    _, right = features(far_places[...])
    store_tiles(rights, atoms // TILE, right)

    @pl.loop(0, pairs.shape[1] // GROUP)
    def _(g):
        parts = []
        for j in range(GROUP):
            p = g * GROUP + j
            u, v = pairs[0, p], pairs[1, p]
            k = jnp.exp(dot(lefts[rows_of(u), :], rights[v]) + SHIFT)
            k = jnp.where(p < count[0], k, 0.0).astype(BF16)
            parts.append((u, dot(k, projected[rows_of(v), :])))
        for t, part in parts:
            ahead[rows_of(t), :] += part


def behind_kernel(
    seat, pairs, count, pairs_below, count_below, cotangent, far, close, places, weight,
    mixed,
    sources, back, lefts, rights, far_places, listed, sem, own_sem,
):
    atoms = cotangent.shape[0]
    tiles = atoms // TILE
    own = pltpu.make_async_copy(cotangent, sources.at[pl.ds(0, atoms)], own_sem)
    own.start()
    packed = sources.at[pl.ds(atoms, ROWS)]

    @pl.when(seat[0] == 0)
    def _():
        pltpu.make_async_copy(far, packed, sem).start()

    @pl.when(seat[0] != 0)
    def _():
        pltpu.make_async_copy(close, packed, sem).start()

    live = jnp.int32(0)
    for p in range(pairs.shape[1]):
        u, v = pairs[0, p], pairs[1, p]
        listed[0, live] = u
        listed[1, live] = jnp.where(v < tiles, v, v - tiles)
        live = live + jnp.where((p < count[0]) & (v < tiles), 1, 0)
        u, v = pairs_below[0, p], pairs_below[1, p]
        listed[0, live] = u + tiles
        listed[1, live] = jnp.where(v < tiles, v, v - tiles)
        live = live + jnp.where((p < count_below[0]) & (v >= tiles), 1, 0)
    for j in range(GROUP):
        listed[0, live + j] = jnp.int32(0)
        listed[1, live + j] = jnp.int32(0)

    left, right = features(places[...])
    lefts[pl.ds(0, atoms), :] = left.T.astype(BF16)
    store_tiles(rights, 0, right)
    back[...] = jnp.zeros_like(back)
    own.wait()
    pltpu.make_async_copy(far, packed, sem).wait()
    unpack_places(packed, far_places)
    left, _ = features(far_places[...])
    lefts[pl.ds(atoms, atoms), :] = left.T.astype(BF16)

    @pl.loop(0, lax.shift_right_logical(live + (GROUP - 1), 2))
    def _(g):
        parts = []
        for j in range(GROUP):
            p = g * GROUP + j
            u, v = listed[0, p], listed[1, p]
            k = jnp.exp(dot(lefts[rows_of(u), :], rights[v]) + SHIFT)
            k = jnp.where(p < live, k, 0.0)
            parts.append((v, dot(k.T.astype(BF16), sources[rows_of(u), :])))
        for t, part in parts:
            back[rows_of(t), :] += part

    mixed[...] = dot(back[...].astype(BF16), weight[...], ((1,), (1,)))


def near_ahead(seat, pairs, count, embedding, far, close, places, weight, wave_filter, atoms_all):
    atoms, channels = embedding.shape
    tiles = atoms // TILE
    hbm = pl.BlockSpec(memory_space=pltpu.HBM)
    return pl.pallas_call(
        functools.partial(ahead_kernel, atoms_all=atoms_all),
        out_shape=(
            jax.ShapeDtypeStruct((atoms, channels), F32),
            jax.ShapeDtypeStruct((8, TILE), F32),
        ),
        in_specs=[SMEM] * 3 + [VMEM, hbm, hbm, VMEM, VMEM, hbm],
        out_specs=(VMEM, VMEM),
        scratch_shapes=[
            pltpu.VMEM((ROWS, channels), BF16),
            pltpu.VMEM((2 * atoms, channels), BF16),
            pltpu.VMEM((atoms, 96), BF16),
            pltpu.VMEM((2 * tiles, 96, TILE), BF16),
            pltpu.VMEM((3, atoms), F32),
            pltpu.VMEM((8, TILE), F32),
            pltpu.SemaphoreType.DMA(()),
            pltpu.SemaphoreType.DMA(()),
        ],
        compiler_params=pltpu.CompilerParams(vmem_limit_bytes=12 << 20),
        cost_estimate=pl.CostEstimate(flops=5 << 30, bytes_accessed=2 << 20, transcendentals=0),
        name="near_ahead",
    )(seat, pairs, count, embedding, in_hbm(far), in_hbm(close), places, weight, in_hbm(wave_filter))


def near_behind(seat, pairs, count, pairs_below, count_below, cotangent, far, close, places, weight):
    atoms, channels = cotangent.shape
    tiles = atoms // TILE
    hbm = pl.BlockSpec(memory_space=pltpu.HBM)
    return pl.pallas_call(
        behind_kernel,
        out_shape=jax.ShapeDtypeStruct((atoms, channels), F32),
        in_specs=[SMEM] * 5 + [hbm] * 3 + [VMEM, VMEM],
        out_specs=VMEM,
        scratch_shapes=[
            pltpu.VMEM((atoms + ROWS, channels), BF16),
            pltpu.VMEM((atoms, channels), F32),
            pltpu.VMEM((2 * atoms, 96), BF16),
            pltpu.VMEM((tiles, 96, TILE), BF16),
            pltpu.VMEM((3, atoms), F32),
            pltpu.SMEM((2, 2 * pairs.shape[1] + GROUP), jnp.int32),
            pltpu.SemaphoreType.DMA(()),
            pltpu.SemaphoreType.DMA(()),
        ],
        compiler_params=pltpu.CompilerParams(vmem_limit_bytes=12 << 20),
        cost_estimate=pl.CostEstimate(flops=5 << 30, bytes_accessed=2 << 20, transcendentals=0),
        name="near_behind",
    )(
        seat, pairs, count, pairs_below, count_below, in_hbm(cotangent), in_hbm(far), in_hbm(close), places, weight
    )


BLOCKS = 4


def final_kernel(
    seat, own, other, table, ahead_far, mixed_far, message_far, grad_far, ahead, mixed, message, grad, matrix, sems, load_sems
):
    channels = message.shape[1]
    size = message.shape[0] // BLOCKS
    loads = [
        [
            pltpu.make_async_copy(far.at[pl.ds(i * size, size)], ref.at[pl.ds(i * size, size)], load_sems.at[side, i])
            for side, (far, ref) in enumerate(((ahead_far, ahead), (mixed_far, mixed)))
        ]
        for i in range(BLOCKS)
    ]
    for both in loads:
        for load in both:
            load.start()
    for half, ref in ((seat[0], own), (1 - seat[0], other)):
        for r in range(0, 64, 2):
            rows = pl.ds(pl.multiple_of(half * 512 + 8 * r, 16), 16)
            for q in range(4):
                pair = [ref[(r + d) * 4 + q].astype(F32) for d in range(2)]
                matrix[rows, 128 * q : 128 * q + 128] = jnp.concatenate(pair, axis=0).astype(BF16)

    stores = []
    for i in range(BLOCKS):
        rows = pl.ds(i * size, size)
        for side, (near, out, far) in enumerate(((ahead, message, message_far), (mixed, grad, grad_far))):
            part = dot(table[rows, :], matrix[:, side * channels : side * channels + channels])
            loads[i][side].wait()
            out[rows, :] = (part + near[rows, :]).astype(BF16)
            store = pltpu.make_async_copy(out.at[rows], far.at[rows], sems.at[side, i])
            store.start()
            stores.append(store)
    for store in stores:
        store.wait()


def final(seat, own, other, table, ahead, mixed):
    shape = ahead.shape
    hbm = pl.BlockSpec(memory_space=pltpu.HBM)
    return pl.pallas_call(
        final_kernel,
        out_shape=(jax.ShapeDtypeStruct(shape, BF16),) * 2,
        in_specs=[SMEM] + [VMEM] * 3 + [hbm] * 2,
        out_specs=(hbm, hbm),
        scratch_shapes=[
            pltpu.VMEM(shape, F32),
            pltpu.VMEM(shape, F32),
            pltpu.VMEM(shape, BF16),
            pltpu.VMEM(shape, BF16),
            pltpu.VMEM((table.shape[1], 2 * shape[1]), BF16),
            pltpu.SemaphoreType.DMA((2, BLOCKS)),
            pltpu.SemaphoreType.DMA((2, BLOCKS)),
        ],
        compiler_params=pltpu.CompilerParams(vmem_limit_bytes=16 << 20),
        cost_estimate=pl.CostEstimate(flops=1 << 30, bytes_accessed=4 << 20, transcendentals=0),
        name="final",
    )(seat, own, other, table, in_hbm(ahead), in_hbm(mixed))


def body(
    embedding, cotangent, fractional, wave_index, tile_pairs, counts, wave_filter, short_weight
):
    devices = math.prod(lax.axis_size(name) for name in FINE)
    atoms_all = embedding.shape[0] * devices
    core, x, y = (lax.axis_index(name).astype(jnp.int32) for name in ("core", "x", "y"))
    z_lo, z_hi = lax.axis_index("z_lo").astype(jnp.int32), lax.axis_index("z_hi").astype(jnp.int32)
    seat = jnp.stack([core, core * 32 + (y & 1) * 16 + x * 4 + z_lo, z_hi & 1])
    swap = [(0, 1), (1, 0)]

    listed = tile_pairs.T
    to_far, to_close = pack(seat[:1], embedding, cotangent, fractional, listed, counts)
    size = math.prod(lax.axis_size(name) for name in FINE)
    far = lax.ppermute(to_far, FINE, [(i, (i + (1 if i % 2 else -1)) % size) for i in range(size)])
    given = partial_sums(1 - seat[:1], wave_index, fractional, embedding, cotangent, True)
    given = lax.ppermute(given, "core", swap)
    kept = partial_sums(seat[:1], wave_index, fractional, embedding, cotangent, False)
    total = add(kept, given)
    chip = lax.all_to_all(total, ("y", "x"), 0, 0, tiled=True)
    close = lax.ppermute(to_close, "core", swap)
    table = tables(wave_index, fractional)
    summed = gather_sum(chip)
    parts = lax.all_to_all(summed, ALONG_Z, 0, 0, tiled=True)
    tail = jnp.where(seat[0] == 0, far[PAIRS:ROWS, :TILE], close[PAIRS:ROWS, :TILE]).astype(jnp.int32)
    pairs_below, count_below = tail[0:2, : listed.shape[1]], tail[LIVE - PAIRS, 0:1]
    ahead, scale = near_ahead(
        seat, listed, counts, embedding, far, close, fractional, short_weight, wave_filter, atoms_all
    )
    mine = lax.all_to_all(coefficients(parts, scale), ALONG_Z, 0, 0, tiled=True)
    mixed = near_behind(
        seat[:1], listed, counts, pairs_below, count_below, cotangent, far, close, fractional, short_weight
    )
    coeffs = lax.all_to_all(copies(mine), ("y", "x"), 0, 0, tiled=True).reshape(256, 8, 128)
    other = lax.ppermute(coeffs, "core", swap)
    return final(seat, coeffs, other, table, ahead, mixed)


def solution(mesh):
    fine = Mesh(mesh.devices.reshape(4, 4, 4, 4, 2), FINE)
    rows, places, one = P(FINE, None), P(None, FINE), P(FINE)
    return jax.shard_map(
        body,
        mesh=fine,
        in_specs=(rows, rows, places, P(), rows, one, P(), P()),
        out_specs=(rows, rows),
        check_vma=False,
    )
```

```python
import functools
import math

import jax
import jax.numpy as jnp
from jax import lax
from jax.experimental import pallas as pl
from jax.experimental.pallas import tpu as pltpu
from jax.sharding import Mesh
from jax.sharding import PartitionSpec as P


TILE = 128
FINE = ("z_lo", "y", "x", "z_hi", "core")
ALONG_Z = ("z_lo", "z_hi")
F32, BF16 = jnp.float32, jnp.bfloat16
VMEM = pl.BlockSpec(memory_space=pltpu.VMEM)
SMEM = pl.BlockSpec(memory_space=pltpu.SMEM)

COS = (
    0.9999999889445764,
    -19.73920446657614,
    64.93911592834654,
    -85.45011342750612,
    60.167429791960785,
    -25.966884612677454,
    6.527705963152031,
)
SIN = (
    6.283185302468581,
    -41.34170039298386,
    81.60513081114435,
    -76.70300555818746,
    42.02585148963868,
    -14.899578436725896,
    3.2377800860428168,
)


def cos_sin(turns):
    r = turns - jnp.floor(turns + 0.5)
    u = r * r
    c, s = COS[-1], SIN[-1]
    for k in COS[-2::-1]:
        c = c * u + k
    for k in SIN[-2::-1]:
        s = s * u + k
    return c, s * r


def dot(a, b, dims=((1,), (0,))):
    return lax.dot_general(a, b, (dims, ((), ())), preferred_element_type=F32)


def padded(rows):
    rows = rows.astype(F32)
    return jnp.concatenate([rows, jnp.zeros((5, rows.shape[1]), F32)], axis=0)


def sums_kernel(seat, waves_far, places_far, left_far, right_far, out, waves, places, left, right, turns, table, sems):
    half, atoms = turns.shape
    mine = pl.ds(pl.multiple_of(seat[0] * half, half), half)
    loads = [
        pltpu.make_async_copy(waves_far.at[:, mine], waves, sems.at[0]),
        pltpu.make_async_copy(places_far, places, sems.at[1]),
        pltpu.make_async_copy(left_far, left, sems.at[2]),
        pltpu.make_async_copy(right_far, right, sems.at[3]),
    ]
    for load in loads:
        load.start()
    loads[0].wait()
    loads[1].wait()
    turns[...] = dot(padded(waves[...]).astype(BF16), padded(places[...]).astype(BF16), ((0,), (0,)))

    @pl.loop(0, half // 16)
    def _(i):
        top = pl.ds(pl.multiple_of(i * 16, 16), 16)
        low = pl.ds(pl.multiple_of(half + i * 16, 16), 16)
        for j in range(atoms // 256):
            cols = pl.ds(j * 256, 256)
            c, s = cos_sin(turns[top, cols])
            table[top, cols] = c.astype(BF16)
            table[low, cols] = s.astype(BF16)

    for side, ref in enumerate((left, right)):
        loads[2 + side].wait()
        for block in range(2):
            part = dot(table[block * half : block * half + half, :], ref[...])
            for r in range(half // 8):
                i, k = divmod(block * (half // 8) + r, 4)
                for q in range(2):
                    out[i, k * 4 + side * 2 + q] = part[8 * r : 8 * r + 8, 128 * q : 128 * q + 128]


def partial_sums(seat, waves, places, left, right, first):
    half, atoms = waves.shape[1] // 2, places.shape[1]
    return pl.pallas_call(
        sums_kernel,
        out_shape=jax.ShapeDtypeStruct((16, 16, 8, 128), F32),
        in_specs=[SMEM] + [pl.BlockSpec(memory_space=pl.ANY)] * 4,
        out_specs=VMEM,
        scratch_shapes=[
            pltpu.VMEM((3, half), waves.dtype),
            pltpu.VMEM(places.shape, BF16),
            pltpu.VMEM(left.shape, BF16),
            pltpu.VMEM(right.shape, BF16),
            pltpu.VMEM((half, atoms), F32),
            pltpu.VMEM((2 * half, atoms), BF16),
            pltpu.SemaphoreType.DMA((4,)),
        ],
        compiler_params=pltpu.CompilerParams(vmem_limit_bytes=12 << 20),
        cost_estimate=pl.CostEstimate(
            flops=4 * half * atoms * 512, bytes_accessed=2 << 20, transcendentals=0
        ),
        name="sums",
    )(seat, *(map(in_hbm, (waves, places)) if first else (waves, places)), in_hbm(left), in_hbm(right))


def add_kernel(a, b, out):
    @pl.loop(0, a.shape[0])
    def _(i):
        out[i] = (a[i] + b[i]).astype(BF16)


def add(a, b):
    return pl.pallas_call(
        add_kernel,
        out_shape=jax.ShapeDtypeStruct(a.shape, BF16),
        in_specs=[VMEM] * 2,
        out_specs=VMEM,
        compiler_params=pltpu.CompilerParams(vmem_limit_bytes=4 << 20),
        name="add",
    )(a, b)


def plane_sum_kernel(a, out):
    for i in range(a.shape[1]):
        total = a[0, i].astype(F32)
        for k in range(1, a.shape[0]):
            total = total + a[k, i].astype(F32)
        mine = total.astype(BF16)
        for k in range(out.shape[0]):
            out[k, i] = mine


def plane_sum(a):
    return pl.pallas_call(
        plane_sum_kernel,
        out_shape=jax.ShapeDtypeStruct(a.shape, BF16),
        in_specs=[VMEM],
        out_specs=VMEM,
        compiler_params=pltpu.CompilerParams(vmem_limit_bytes=4 << 20),
        name="plane_sum",
    )(a)


def coefficients_kernel(a, scale, out):
    for i in range(a.shape[1]):
        total = a[0, i].astype(F32)
        for k in range(1, a.shape[0]):
            total = total + a[k, i].astype(F32)
        mine = (total * scale[i]).astype(BF16)
        for k in range(out.shape[0]):
            out[k, i] = mine


def coefficients(a, scale):
    return pl.pallas_call(
        coefficients_kernel,
        out_shape=jax.ShapeDtypeStruct(a.shape, BF16),
        in_specs=[VMEM] * 2,
        out_specs=VMEM,
        compiler_params=pltpu.CompilerParams(vmem_limit_bytes=4 << 20),
        name="coefficients",
    )(a, scale)


def table_kernel(waves, places, table, turns):
    atoms, count = turns.shape
    half = count // 2
    turns[...] = dot(padded(places[...]).astype(BF16), padded(waves[...]).astype(BF16), ((0,), (0,)))

    @pl.loop(0, atoms // 16)
    def _(i):
        rows = pl.ds(pl.multiple_of(i * 16, 16), 16)
        for j in range(2):
            c, s = cos_sin(turns[rows, j * half : j * half + half])
            table[rows, 2 * j * half : (2 * j + 1) * half] = c.astype(BF16)
            table[rows, (2 * j + 1) * half : (2 * j + 2) * half] = s.astype(BF16)


def tables(waves, places):
    atoms, count = places.shape[1], waves.shape[1]
    return pl.pallas_call(
        table_kernel,
        out_shape=jax.ShapeDtypeStruct((atoms, 2 * count), BF16),
        in_specs=[VMEM] * 2,
        out_specs=VMEM,
        scratch_shapes=[pltpu.VMEM((atoms, count), F32)],
        compiler_params=pltpu.CompilerParams(vmem_limit_bytes=8 << 20),
        cost_estimate=pl.CostEstimate(flops=6 << 30, bytes_accessed=2 << 20, transcendentals=0),
        name="table",
    )(waves, places)


def thirds(value):
    a = value.astype(BF16).astype(F32)
    b = (value - a).astype(BF16).astype(F32)
    return a, b, value - a - b


def features(places):
    coords = padded(places)
    live = lax.broadcasted_iota(jnp.int32, coords.shape, 0) < 3
    parts = [thirds(jnp.where(live, v, 0.0)) for v in cos_sin(coords)]
    left = jnp.concatenate([p[k] for k in (0, 0, 1, 1, 0, 2) for p in parts], axis=0)
    right = jnp.concatenate([p[k] for k in (0, 1, 0, 1, 2, 0) for p in parts], axis=0)
    return left, right


PLACES, PAIRS, LIVE, ROWS = 1024, 1040, 1048, 1056


def pack_kernel(seat, embedding, cotangent, places_far, pairs_far, count, far, close, places, pairs, sems):
    atoms = embedding.shape[0]
    small = [
        pltpu.make_async_copy(places_far, places, sems.at[2]),
        pltpu.make_async_copy(pairs_far, pairs, sems.at[3]),
    ]
    for load in small:
        load.start()

    def both(forward, backward):
        a = pltpu.make_async_copy(embedding, backward.at[pl.ds(0, atoms)], sems.at[0])
        b = pltpu.make_async_copy(cotangent, forward.at[pl.ds(0, atoms)], sems.at[1])
        a.start()
        b.start()
        return a, b

    @pl.when(seat[0] == 0)
    def _():
        both(close, far)

    @pl.when(seat[0] != 0)
    def _():
        both(far, close)

    width = far.shape[1]
    for load in small:
        load.wait()
    coords = places[...].astype(F32)
    rows = [coords[d : d + 1, k * width : k * width + width] for d in range(3) for k in range(4)]
    rows = jnp.concatenate([*rows, jnp.zeros((4, width), F32)], axis=0).astype(BF16)
    listed = jnp.concatenate([pairs[...].astype(F32), jnp.zeros((2, width - pairs.shape[1]), F32)], axis=1)
    listed = jnp.concatenate([listed, jnp.zeros((6, width), F32)], axis=0)
    tail = jnp.concatenate([listed, jnp.full((8, width), count[0], jnp.int32).astype(F32)], axis=0).astype(BF16)
    for ref in (far, close):
        ref[PLACES:PAIRS, :] = rows
        ref[PAIRS:ROWS, :] = tail
    pltpu.make_async_copy(embedding, far.at[pl.ds(0, atoms)], sems.at[0]).wait()
    pltpu.make_async_copy(cotangent, close.at[pl.ds(0, atoms)], sems.at[1]).wait()


def pack(seat, embedding, cotangent, places, pairs, count):
    hbm = pl.BlockSpec(memory_space=pltpu.HBM)
    return pl.pallas_call(
        pack_kernel,
        out_shape=(jax.ShapeDtypeStruct((ROWS, embedding.shape[1]), BF16),) * 2,
        in_specs=[SMEM, hbm, hbm, hbm, hbm, SMEM],
        out_specs=(VMEM, VMEM),
        scratch_shapes=[
            pltpu.VMEM(places.shape, BF16),
            pltpu.VMEM(pairs.shape, pairs.dtype),
            pltpu.SemaphoreType.DMA((4,)),
        ],
        compiler_params=pltpu.CompilerParams(vmem_limit_bytes=4 << 20),
        name="pack",
    )(seat, *map(in_hbm, (embedding, cotangent, places, pairs)), count)


def in_hbm(value):
    return pltpu.with_memory_space_constraint(value, pltpu.HBM)


GROUP = 4
SHIFT = -3.0 - 0.5 * math.log(TILE)


def rows_of(t):
    return pl.ds(pl.multiple_of(t * TILE, TILE), TILE)


def unpack_places(packed, places):
    width = packed.shape[1]
    rows = packed[PLACES:PAIRS, :].astype(F32)
    for d in range(3):
        for k in range(4):
            places[d : d + 1, k * width : k * width + width] = rows[4 * d + k : 4 * d + k + 1]


def store_tiles(rights, first, right):
    for t in range(right.shape[1] // TILE):
        rights[first + t] = right[:, t * TILE : t * TILE + TILE].astype(BF16)


def ahead_kernel(
    seat, pairs, count, embedding, far, close, places, weight, wave_filter,
    ahead, scale,
    above, projected, lefts, rights, far_places, tile, sem, tile_sem, *, atoms_all,
):
    atoms = embedding.shape[0]
    mine = wave_filter.at[pl.ds(pl.multiple_of(seat[1] * 32, 32), 32)]
    filtering = pltpu.make_async_copy(mine, tile, tile_sem)
    filtering.start()

    @pl.when(seat[0] == 0)
    def _():
        pltpu.make_async_copy(close, above, sem).start()

    @pl.when(seat[0] != 0)
    def _():
        pltpu.make_async_copy(far, above, sem).start()

    projected[pl.ds(0, atoms), :] = dot(embedding[...], weight[...]).astype(BF16)
    left, right = features(places[...])
    lefts[...] = left.T.astype(BF16)
    store_tiles(rights, 0, right)
    ahead[...] = jnp.zeros_like(ahead)
    filtering.wait()
    for i in range(scale.shape[0]):
        rows, cols = i // 4 * 8, i % 2 * TILE
        scale[i] = tile[rows : rows + 8, cols : cols + TILE] * (1.0 / math.sqrt(atoms_all))
    pltpu.make_async_copy(far, above, sem).wait()
    projected[pl.ds(atoms, atoms), :] = dot(above[pl.ds(0, atoms), :], weight[...]).astype(BF16)
    unpack_places(above, far_places)
    _, right = features(far_places[...])
    store_tiles(rights, atoms // TILE, right)

    @pl.loop(0, pairs.shape[1] // GROUP)
    def _(g):
        parts = []
        for j in range(GROUP):
            p = g * GROUP + j
            u, v = pairs[0, p], pairs[1, p]
            k = jnp.exp(dot(lefts[rows_of(u), :], rights[v]) + SHIFT)
            k = jnp.where(p < count[0], k, 0.0).astype(BF16)
            parts.append((u, dot(k, projected[rows_of(v), :])))
        for t, part in parts:
            ahead[rows_of(t), :] += part


def behind_kernel(
    seat, pairs, count, pairs_below, count_below, cotangent, far, close, places, weight,
    mixed,
    sources, back, lefts, rights, far_places, listed, sem, own_sem,
):
    atoms = cotangent.shape[0]
    tiles = atoms // TILE
    own = pltpu.make_async_copy(cotangent, sources.at[pl.ds(0, atoms)], own_sem)
    own.start()
    packed = sources.at[pl.ds(atoms, ROWS)]

    @pl.when(seat[0] == 0)
    def _():
        pltpu.make_async_copy(far, packed, sem).start()

    @pl.when(seat[0] != 0)
    def _():
        pltpu.make_async_copy(close, packed, sem).start()

    live = jnp.int32(0)
    for p in range(pairs.shape[1]):
        u, v = pairs[0, p], pairs[1, p]
        listed[0, live] = u
        listed[1, live] = jnp.where(v < tiles, v, v - tiles)
        live = live + jnp.where((p < count[0]) & (v < tiles), 1, 0)
        u, v = pairs_below[0, p], pairs_below[1, p]
        listed[0, live] = u + tiles
        listed[1, live] = jnp.where(v < tiles, v, v - tiles)
        live = live + jnp.where((p < count_below[0]) & (v >= tiles), 1, 0)
    for j in range(GROUP):
        listed[0, live + j] = jnp.int32(0)
        listed[1, live + j] = jnp.int32(0)

    left, right = features(places[...])
    lefts[pl.ds(0, atoms), :] = left.T.astype(BF16)
    store_tiles(rights, 0, right)
    back[...] = jnp.zeros_like(back)
    own.wait()
    pltpu.make_async_copy(far, packed, sem).wait()
    unpack_places(packed, far_places)
    left, _ = features(far_places[...])
    lefts[pl.ds(atoms, atoms), :] = left.T.astype(BF16)

    @pl.loop(0, lax.shift_right_logical(live + (GROUP - 1), 2))
    def _(g):
        parts = []
        for j in range(GROUP):
            p = g * GROUP + j
            u, v = listed[0, p], listed[1, p]
            k = jnp.exp(dot(lefts[rows_of(u), :], rights[v]) + SHIFT)
            k = jnp.where(p < live, k, 0.0)
            parts.append((v, dot(k.T.astype(BF16), sources[rows_of(u), :])))
        for t, part in parts:
            back[rows_of(t), :] += part

    mixed[...] = dot(back[...].astype(BF16), weight[...], ((1,), (1,)))


def near_ahead(seat, pairs, count, embedding, far, close, places, weight, wave_filter, atoms_all):
    atoms, channels = embedding.shape
    tiles = atoms // TILE
    hbm = pl.BlockSpec(memory_space=pltpu.HBM)
    return pl.pallas_call(
        functools.partial(ahead_kernel, atoms_all=atoms_all),
        out_shape=(
            jax.ShapeDtypeStruct((atoms, channels), F32),
            jax.ShapeDtypeStruct((16, 8, TILE), F32),
        ),
        in_specs=[SMEM] * 3 + [VMEM, hbm, hbm, VMEM, VMEM, hbm],
        out_specs=(VMEM, VMEM),
        scratch_shapes=[
            pltpu.VMEM((ROWS, channels), BF16),
            pltpu.VMEM((2 * atoms, channels), BF16),
            pltpu.VMEM((atoms, 96), BF16),
            pltpu.VMEM((2 * tiles, 96, TILE), BF16),
            pltpu.VMEM((3, atoms), F32),
            pltpu.VMEM((32, channels), F32),
            pltpu.SemaphoreType.DMA(()),
            pltpu.SemaphoreType.DMA(()),
        ],
        compiler_params=pltpu.CompilerParams(vmem_limit_bytes=12 << 20),
        cost_estimate=pl.CostEstimate(flops=5 << 30, bytes_accessed=2 << 20, transcendentals=0),
        name="near_ahead",
    )(seat, pairs, count, embedding, in_hbm(far), in_hbm(close), places, weight, in_hbm(wave_filter))


def near_behind(seat, pairs, count, pairs_below, count_below, cotangent, far, close, places, weight):
    atoms, channels = cotangent.shape
    tiles = atoms // TILE
    hbm = pl.BlockSpec(memory_space=pltpu.HBM)
    return pl.pallas_call(
        behind_kernel,
        out_shape=jax.ShapeDtypeStruct((atoms, channels), F32),
        in_specs=[SMEM] * 5 + [hbm] * 3 + [VMEM, VMEM],
        out_specs=VMEM,
        scratch_shapes=[
            pltpu.VMEM((atoms + ROWS, channels), BF16),
            pltpu.VMEM((atoms, channels), F32),
            pltpu.VMEM((2 * atoms, 96), BF16),
            pltpu.VMEM((tiles, 96, TILE), BF16),
            pltpu.VMEM((3, atoms), F32),
            pltpu.SMEM((2, 2 * pairs.shape[1] + GROUP), jnp.int32),
            pltpu.SemaphoreType.DMA(()),
            pltpu.SemaphoreType.DMA(()),
        ],
        compiler_params=pltpu.CompilerParams(vmem_limit_bytes=12 << 20),
        cost_estimate=pl.CostEstimate(flops=5 << 30, bytes_accessed=2 << 20, transcendentals=0),
        name="near_behind",
    )(
        seat, pairs, count, pairs_below, count_below, in_hbm(cotangent), in_hbm(far), in_hbm(close), places, weight
    )


def final_kernel(seat, own, other, table, ahead, mixed, message, grad, matrix):
    channels = message.shape[1]

    @pl.when(pl.program_id(0) == 0)
    def _():
        for half, ref in ((seat[0], own), (1 - seat[0], other)):
            for r in range(0, 64, 2):
                rows = pl.ds(pl.multiple_of(half * 512 + 8 * r, 16), 16)
                for q in range(4):
                    pair = [ref[(r + d) * 4 + q].astype(F32) for d in range(2)]
                    matrix[rows, 128 * q : 128 * q + 128] = jnp.concatenate(pair, axis=0).astype(BF16)

    message[...] = (dot(table[...], matrix[:, :channels]) + ahead[...]).astype(BF16)
    grad[...] = (dot(table[...], matrix[:, channels:]) + mixed[...]).astype(BF16)


def final(seat, own, other, table, ahead, mixed, steps=2):
    atoms, channels = ahead.shape
    rows = atoms // steps
    block = pl.BlockSpec((rows, channels), lambda i: (i, 0))
    whole = pl.BlockSpec(own.shape, lambda i: (0, 0, 0), pipeline_mode=pl.Buffered(1))
    return pl.pallas_call(
        final_kernel,
        grid=(steps,),
        out_shape=(jax.ShapeDtypeStruct((atoms, channels), BF16),) * 2,
        in_specs=[
            SMEM,
            whole,
            whole,
            pl.BlockSpec((rows, table.shape[1]), lambda i: (i, 0)),
            block,
            block,
        ],
        out_specs=(block, block),
        scratch_shapes=[pltpu.VMEM((table.shape[1], 2 * channels), BF16)],
        compiler_params=pltpu.CompilerParams(vmem_limit_bytes=16 << 20),
        cost_estimate=pl.CostEstimate(flops=1 << 30, bytes_accessed=4 << 20, transcendentals=0),
        name="final",
    )(seat, own, other, table, in_hbm(ahead), in_hbm(mixed))


def body(
    embedding, cotangent, fractional, wave_index, tile_pairs, counts, wave_filter, short_weight
):
    devices = math.prod(lax.axis_size(name) for name in FINE)
    atoms_all = embedding.shape[0] * devices
    core, x, y = (lax.axis_index(name).astype(jnp.int32) for name in ("core", "x", "y"))
    seat = jnp.stack([core, core * 8 + (y & 1) * 4 + x])
    swap = [(0, 1), (1, 0)]

    listed = tile_pairs.T
    to_far, to_close = pack(seat[:1], embedding, cotangent, fractional, listed, counts)
    size = math.prod(lax.axis_size(name) for name in FINE)
    far = lax.ppermute(to_far, FINE, [(i, (i + (1 if i % 2 else -1)) % size) for i in range(size)])
    given = partial_sums(1 - seat[:1], wave_index, fractional, embedding, cotangent, True)
    given = lax.ppermute(given, "core", swap)
    kept = partial_sums(seat[:1], wave_index, fractional, embedding, cotangent, False)
    total = add(kept, given)
    chip = lax.all_to_all(total, ("y", "x"), 0, 0, tiled=True)
    close = lax.ppermute(to_close, "core", swap)
    table = tables(wave_index, fractional)
    summed = plane_sum(chip)
    parts = lax.all_to_all(summed, ALONG_Z, 0, 0, tiled=True)
    tail = jnp.where(seat[0] == 0, far[PAIRS:ROWS, :TILE], close[PAIRS:ROWS, :TILE]).astype(jnp.int32)
    pairs_below, count_below = tail[0:2, : listed.shape[1]], tail[LIVE - PAIRS, 0:1]
    ahead, scale = near_ahead(
        seat, listed, counts, embedding, far, close, fractional, short_weight, wave_filter, atoms_all
    )
    mixed = near_behind(
        seat[:1], listed, counts, pairs_below, count_below, cotangent, far, close, fractional, short_weight
    )
    coeffs = lax.all_to_all(coefficients(parts, scale), ("y", "x"), 0, 0, tiled=True).reshape(256, 8, 128)
    other = lax.ppermute(coeffs, "core", swap)
    return final(seat, coeffs, other, table, ahead, mixed)


def solution(mesh):
    fine = Mesh(mesh.devices.reshape(4, 4, 4, 4, 2), FINE)
    rows, places, one = P(FINE, None), P(None, FINE), P(FINE)
    return jax.shard_map(
        body,
        mesh=fine,
        in_specs=(rows, rows, places, P(), rows, one, P(), P()),
        out_specs=(rows, rows),
        check_vma=False,
    )
```

```python
import functools
import math

import jax
import jax.numpy as jnp
from jax import lax
from jax.experimental import pallas as pl
from jax.experimental.pallas import tpu as pltpu
from jax.sharding import Mesh
from jax.sharding import PartitionSpec as P


TILE = 128
FINE = ("z_lo", "y", "x", "z_hi", "core")
ALONG_Z = ("z_lo", "z_hi")
F32, BF16 = jnp.float32, jnp.bfloat16
VMEM = pl.BlockSpec(memory_space=pltpu.VMEM)
SMEM = pl.BlockSpec(memory_space=pltpu.SMEM)

COS = (
    0.9999999889445764,
    -19.73920446657614,
    64.93911592834654,
    -85.45011342750612,
    60.167429791960785,
    -25.966884612677454,
    6.527705963152031,
)
SIN = (
    6.283185302468581,
    -41.34170039298386,
    81.60513081114435,
    -76.70300555818746,
    42.02585148963868,
    -14.899578436725896,
    3.2377800860428168,
)


def cos_sin(turns):
    r = turns - jnp.floor(turns + 0.5)
    u = r * r
    c, s = COS[-1], SIN[-1]
    for k in COS[-2::-1]:
        c = c * u + k
    for k in SIN[-2::-1]:
        s = s * u + k
    return c, s * r


def dot(a, b, dims=((1,), (0,))):
    return lax.dot_general(a, b, (dims, ((), ())), preferred_element_type=F32)


def padded(rows):
    rows = rows.astype(F32)
    return jnp.concatenate([rows, jnp.zeros((5, rows.shape[1]), F32)], axis=0)


def sums_kernel(seat, waves_far, places_far, left_far, right_far, out, waves, places, left, right, turns, table, sems):
    half, atoms = turns.shape
    mine = pl.ds(pl.multiple_of(seat[0] * half, half), half)
    loads = [
        pltpu.make_async_copy(waves_far.at[:, mine], waves, sems.at[0]),
        pltpu.make_async_copy(places_far, places, sems.at[1]),
        pltpu.make_async_copy(left_far, left, sems.at[2]),
        pltpu.make_async_copy(right_far, right, sems.at[3]),
    ]
    for load in loads:
        load.start()
    loads[0].wait()
    loads[1].wait()
    turns[...] = dot(padded(waves[...]).astype(BF16), padded(places[...]).astype(BF16), ((0,), (0,)))

    @pl.loop(0, half // 16)
    def _(i):
        top = pl.ds(pl.multiple_of(i * 16, 16), 16)
        low = pl.ds(pl.multiple_of(half + i * 16, 16), 16)
        for j in range(atoms // 256):
            cols = pl.ds(j * 256, 256)
            c, s = cos_sin(turns[top, cols])
            table[top, cols] = c.astype(BF16)
            table[low, cols] = s.astype(BF16)

    for side, ref in enumerate((left, right)):
        loads[2 + side].wait()
        for block in range(2):
            part = dot(table[block * half : block * half + half, :], ref[...])
            for r in range(half // 8):
                i, k = divmod(block * (half // 8) + r, 4)
                for q in range(2):
                    out[i, k * 4 + side * 2 + q] = part[8 * r : 8 * r + 8, 128 * q : 128 * q + 128]


def partial_sums(seat, waves, places, left, right, first):
    half, atoms = waves.shape[1] // 2, places.shape[1]
    return pl.pallas_call(
        sums_kernel,
        out_shape=jax.ShapeDtypeStruct((16, 16, 8, 128), F32),
        in_specs=[SMEM] + [pl.BlockSpec(memory_space=pl.ANY)] * 4,
        out_specs=VMEM,
        scratch_shapes=[
            pltpu.VMEM((3, half), waves.dtype),
            pltpu.VMEM(places.shape, BF16),
            pltpu.VMEM(left.shape, BF16),
            pltpu.VMEM(right.shape, BF16),
            pltpu.VMEM((half, atoms), F32),
            pltpu.VMEM((2 * half, atoms), BF16),
            pltpu.SemaphoreType.DMA((4,)),
        ],
        compiler_params=pltpu.CompilerParams(vmem_limit_bytes=12 << 20),
        cost_estimate=pl.CostEstimate(
            flops=4 * half * atoms * 512, bytes_accessed=2 << 20, transcendentals=0
        ),
        name="sums",
    )(seat, *(map(in_hbm, (waves, places)) if first else (waves, places)), in_hbm(left), in_hbm(right))


def add_kernel(a, b, out):
    @pl.loop(0, a.shape[0])
    def _(i):
        out[i] = (a[i] + b[i]).astype(BF16)


def add(a, b):
    return pl.pallas_call(
        add_kernel,
        out_shape=jax.ShapeDtypeStruct(a.shape, BF16),
        in_specs=[VMEM] * 2,
        out_specs=VMEM,
        compiler_params=pltpu.CompilerParams(vmem_limit_bytes=4 << 20),
        name="add",
    )(a, b)


def plane_sum_kernel(a, out):
    for i in range(a.shape[1]):
        total = a[0, i].astype(F32)
        for k in range(1, a.shape[0]):
            total = total + a[k, i].astype(F32)
        mine = total.astype(BF16)
        for k in range(out.shape[0]):
            out[k, i] = mine


def plane_sum(a):
    return pl.pallas_call(
        plane_sum_kernel,
        out_shape=jax.ShapeDtypeStruct(a.shape, BF16),
        in_specs=[VMEM],
        out_specs=VMEM,
        compiler_params=pltpu.CompilerParams(vmem_limit_bytes=4 << 20),
        name="plane_sum",
    )(a)


def coefficients_kernel(a, scale, out):
    for i in range(a.shape[1]):
        total = a[0, i].astype(F32)
        for k in range(1, a.shape[0]):
            total = total + a[k, i].astype(F32)
        mine = (total * scale[i]).astype(BF16)
        for k in range(out.shape[0]):
            out[k, i] = mine


def coefficients(a, scale):
    return pl.pallas_call(
        coefficients_kernel,
        out_shape=jax.ShapeDtypeStruct(a.shape, BF16),
        in_specs=[VMEM] * 2,
        out_specs=VMEM,
        compiler_params=pltpu.CompilerParams(vmem_limit_bytes=4 << 20),
        name="coefficients",
    )(a, scale)


def table_kernel(waves, places, table, turns):
    atoms, count = turns.shape
    half = count // 2
    turns[...] = dot(padded(places[...]).astype(BF16), padded(waves[...]).astype(BF16), ((0,), (0,)))

    @pl.loop(0, atoms // 16)
    def _(i):
        rows = pl.ds(pl.multiple_of(i * 16, 16), 16)
        for j in range(2):
            c, s = cos_sin(turns[rows, j * half : j * half + half])
            table[rows, 2 * j * half : (2 * j + 1) * half] = c.astype(BF16)
            table[rows, (2 * j + 1) * half : (2 * j + 2) * half] = s.astype(BF16)


def tables(waves, places):
    atoms, count = places.shape[1], waves.shape[1]
    return pl.pallas_call(
        table_kernel,
        out_shape=jax.ShapeDtypeStruct((atoms, 2 * count), BF16),
        in_specs=[VMEM] * 2,
        out_specs=VMEM,
        scratch_shapes=[pltpu.VMEM((atoms, count), F32)],
        compiler_params=pltpu.CompilerParams(vmem_limit_bytes=8 << 20),
        cost_estimate=pl.CostEstimate(flops=6 << 30, bytes_accessed=2 << 20, transcendentals=0),
        name="table",
    )(waves, places)


def thirds(value):
    a = value.astype(BF16).astype(F32)
    b = (value - a).astype(BF16).astype(F32)
    return a, b, value - a - b


def features(places):
    coords = padded(places)
    live = lax.broadcasted_iota(jnp.int32, coords.shape, 0) < 3
    parts = [thirds(jnp.where(live, v, 0.0)) for v in cos_sin(coords)]
    left = jnp.concatenate([p[k] for k in (0, 0, 1, 1, 0, 2) for p in parts], axis=0)
    right = jnp.concatenate([p[k] for k in (0, 1, 0, 1, 2, 0) for p in parts], axis=0)
    return left, right


PLACES, PAIRS, LIVE, ROWS = 1024, 1040, 1048, 1056


def pack_kernel(which, embedding, cotangent, places_far, pairs_far, count, out, places, pairs, sems):
    atoms = embedding.shape[0]
    small = [
        pltpu.make_async_copy(places_far, places, sems.at[1]),
        pltpu.make_async_copy(pairs_far, pairs, sems.at[2]),
    ]
    for load in small:
        load.start()

    @pl.when(which[0] == 0)
    def _():
        pltpu.make_async_copy(embedding, out.at[pl.ds(0, atoms)], sems.at[0]).start()

    @pl.when(which[0] != 0)
    def _():
        pltpu.make_async_copy(cotangent, out.at[pl.ds(0, atoms)], sems.at[0]).start()

    width = out.shape[1]
    for load in small:
        load.wait()
    coords = places[...].astype(F32)
    rows = [coords[d : d + 1, k * width : k * width + width] for d in range(3) for k in range(4)]
    rows = jnp.concatenate([*rows, jnp.zeros((4, width), F32)], axis=0).astype(BF16)
    listed = jnp.concatenate([pairs[...].astype(F32), jnp.zeros((2, width - pairs.shape[1]), F32)], axis=1)
    listed = jnp.concatenate([listed, jnp.zeros((6, width), F32)], axis=0)
    tail = jnp.concatenate([listed, jnp.full((8, width), count[0], jnp.int32).astype(F32)], axis=0).astype(BF16)
    out[PLACES:PAIRS, :] = rows
    out[PAIRS:ROWS, :] = tail
    pltpu.make_async_copy(embedding, out.at[pl.ds(0, atoms)], sems.at[0]).wait()


def pack(which, embedding, cotangent, places, pairs, count):
    hbm = pl.BlockSpec(memory_space=pltpu.HBM)
    return pl.pallas_call(
        pack_kernel,
        out_shape=jax.ShapeDtypeStruct((ROWS, embedding.shape[1]), BF16),
        in_specs=[SMEM, hbm, hbm, hbm, hbm, SMEM],
        out_specs=VMEM,
        scratch_shapes=[
            pltpu.VMEM(places.shape, BF16),
            pltpu.VMEM(pairs.shape, pairs.dtype),
            pltpu.SemaphoreType.DMA((3,)),
        ],
        compiler_params=pltpu.CompilerParams(vmem_limit_bytes=4 << 20),
        name="pack",
    )(which, *map(in_hbm, (embedding, cotangent, places, pairs)), count)


def in_hbm(value):
    return pltpu.with_memory_space_constraint(value, pltpu.HBM)


GROUP = 4
SHIFT = -3.0 - 0.5 * math.log(TILE)


def rows_of(t):
    return pl.ds(pl.multiple_of(t * TILE, TILE), TILE)


def unpack_places(packed, places):
    width = packed.shape[1]
    rows = packed[PLACES:PAIRS, :].astype(F32)
    for d in range(3):
        for k in range(4):
            places[d : d + 1, k * width : k * width + width] = rows[4 * d + k : 4 * d + k + 1]


def store_tiles(rights, first, right):
    for t in range(right.shape[1] // TILE):
        rights[first + t] = right[:, t * TILE : t * TILE + TILE].astype(BF16)


def ahead_kernel(
    seat, pairs, count, embedding, far, close, places, weight, wave_filter,
    ahead, scale,
    above, projected, lefts, rights, far_places, tile, sem, tile_sem, *, atoms_all,
):
    atoms = embedding.shape[0]
    mine = wave_filter.at[pl.ds(pl.multiple_of(seat[1] * 32, 32), 32)]
    filtering = pltpu.make_async_copy(mine, tile, tile_sem)
    filtering.start()

    @pl.when(seat[0] == 0)
    def _():
        pltpu.make_async_copy(close, above, sem).start()

    @pl.when(seat[0] != 0)
    def _():
        pltpu.make_async_copy(far, above, sem).start()

    projected[pl.ds(0, atoms), :] = dot(embedding[...], weight[...]).astype(BF16)
    left, right = features(places[...])
    lefts[...] = left.T.astype(BF16)
    store_tiles(rights, 0, right)
    ahead[...] = jnp.zeros_like(ahead)
    filtering.wait()
    for i in range(scale.shape[0]):
        rows, cols = i // 4 * 8, i % 2 * TILE
        scale[i] = tile[rows : rows + 8, cols : cols + TILE] * (1.0 / math.sqrt(atoms_all))
    pltpu.make_async_copy(far, above, sem).wait()
    projected[pl.ds(atoms, atoms), :] = dot(above[pl.ds(0, atoms), :], weight[...]).astype(BF16)
    unpack_places(above, far_places)
    _, right = features(far_places[...])
    store_tiles(rights, atoms // TILE, right)

    @pl.loop(0, pairs.shape[1] // GROUP)
    def _(g):
        parts = []
        for j in range(GROUP):
            p = g * GROUP + j
            u, v = pairs[0, p], pairs[1, p]
            k = jnp.exp(dot(lefts[rows_of(u), :], rights[v]) + SHIFT)
            k = jnp.where(p < count[0], k, 0.0).astype(BF16)
            parts.append((u, dot(k, projected[rows_of(v), :])))
        for t, part in parts:
            ahead[rows_of(t), :] += part


def behind_kernel(
    seat, pairs, count, pairs_below, count_below, cotangent, far, close, places, weight,
    mixed,
    sources, back, lefts, rights, far_places, listed, sem, own_sem,
):
    atoms = cotangent.shape[0]
    tiles = atoms // TILE
    own = pltpu.make_async_copy(cotangent, sources.at[pl.ds(0, atoms)], own_sem)
    own.start()
    packed = sources.at[pl.ds(atoms, ROWS)]

    @pl.when(seat[0] == 0)
    def _():
        pltpu.make_async_copy(far, packed, sem).start()

    @pl.when(seat[0] != 0)
    def _():
        pltpu.make_async_copy(close, packed, sem).start()

    live = jnp.int32(0)
    for p in range(pairs.shape[1]):
        u, v = pairs[0, p], pairs[1, p]
        listed[0, live] = u
        listed[1, live] = jnp.where(v < tiles, v, v - tiles)
        live = live + jnp.where((p < count[0]) & (v < tiles), 1, 0)
        u, v = pairs_below[0, p], pairs_below[1, p]
        listed[0, live] = u + tiles
        listed[1, live] = jnp.where(v < tiles, v, v - tiles)
        live = live + jnp.where((p < count_below[0]) & (v >= tiles), 1, 0)
    for j in range(GROUP):
        listed[0, live + j] = jnp.int32(0)
        listed[1, live + j] = jnp.int32(0)

    left, right = features(places[...])
    lefts[pl.ds(0, atoms), :] = left.T.astype(BF16)
    store_tiles(rights, 0, right)
    back[...] = jnp.zeros_like(back)
    own.wait()
    pltpu.make_async_copy(far, packed, sem).wait()
    unpack_places(packed, far_places)
    left, _ = features(far_places[...])
    lefts[pl.ds(atoms, atoms), :] = left.T.astype(BF16)

    @pl.loop(0, lax.shift_right_logical(live + (GROUP - 1), 2))
    def _(g):
        parts = []
        for j in range(GROUP):
            p = g * GROUP + j
            u, v = listed[0, p], listed[1, p]
            k = jnp.exp(dot(lefts[rows_of(u), :], rights[v]) + SHIFT)
            k = jnp.where(p < live, k, 0.0)
            parts.append((v, dot(k.T.astype(BF16), sources[rows_of(u), :])))
        for t, part in parts:
            back[rows_of(t), :] += part

    mixed[...] = dot(back[...].astype(BF16), weight[...], ((1,), (1,)))


def near_ahead(seat, pairs, count, embedding, far, close, places, weight, wave_filter, atoms_all):
    atoms, channels = embedding.shape
    tiles = atoms // TILE
    hbm = pl.BlockSpec(memory_space=pltpu.HBM)
    return pl.pallas_call(
        functools.partial(ahead_kernel, atoms_all=atoms_all),
        out_shape=(
            jax.ShapeDtypeStruct((atoms, channels), F32),
            jax.ShapeDtypeStruct((16, 8, TILE), F32),
        ),
        in_specs=[SMEM] * 3 + [VMEM, hbm, hbm, VMEM, VMEM, hbm],
        out_specs=(VMEM, VMEM),
        scratch_shapes=[
            pltpu.VMEM((ROWS, channels), BF16),
            pltpu.VMEM((2 * atoms, channels), BF16),
            pltpu.VMEM((atoms, 96), BF16),
            pltpu.VMEM((2 * tiles, 96, TILE), BF16),
            pltpu.VMEM((3, atoms), F32),
            pltpu.VMEM((32, channels), F32),
            pltpu.SemaphoreType.DMA(()),
            pltpu.SemaphoreType.DMA(()),
        ],
        compiler_params=pltpu.CompilerParams(vmem_limit_bytes=12 << 20),
        cost_estimate=pl.CostEstimate(flops=5 << 30, bytes_accessed=2 << 20, transcendentals=0),
        name="near_ahead",
    )(seat, pairs, count, embedding, in_hbm(far), in_hbm(close), places, weight, in_hbm(wave_filter))


def near_behind(seat, pairs, count, pairs_below, count_below, cotangent, far, close, places, weight):
    atoms, channels = cotangent.shape
    tiles = atoms // TILE
    hbm = pl.BlockSpec(memory_space=pltpu.HBM)
    return pl.pallas_call(
        behind_kernel,
        out_shape=jax.ShapeDtypeStruct((atoms, channels), F32),
        in_specs=[SMEM] * 5 + [hbm] * 3 + [VMEM, VMEM],
        out_specs=VMEM,
        scratch_shapes=[
            pltpu.VMEM((atoms + ROWS, channels), BF16),
            pltpu.VMEM((atoms, channels), F32),
            pltpu.VMEM((2 * atoms, 96), BF16),
            pltpu.VMEM((tiles, 96, TILE), BF16),
            pltpu.VMEM((3, atoms), F32),
            pltpu.SMEM((2, 2 * pairs.shape[1] + GROUP), jnp.int32),
            pltpu.SemaphoreType.DMA(()),
            pltpu.SemaphoreType.DMA(()),
        ],
        compiler_params=pltpu.CompilerParams(vmem_limit_bytes=12 << 20),
        cost_estimate=pl.CostEstimate(flops=5 << 30, bytes_accessed=2 << 20, transcendentals=0),
        name="near_behind",
    )(
        seat, pairs, count, pairs_below, count_below, in_hbm(cotangent), in_hbm(far), in_hbm(close), places, weight
    )


def final_kernel(seat, own, other, table, ahead, mixed, message, grad, matrix):
    channels = message.shape[1]

    @pl.when(pl.program_id(0) == 0)
    def _():
        for half, ref in ((seat[0], own), (1 - seat[0], other)):
            for r in range(0, 64, 2):
                rows = pl.ds(pl.multiple_of(half * 512 + 8 * r, 16), 16)
                for q in range(4):
                    pair = [ref[(r + d) * 4 + q].astype(F32) for d in range(2)]
                    matrix[rows, 128 * q : 128 * q + 128] = jnp.concatenate(pair, axis=0).astype(BF16)

    message[...] = (dot(table[...], matrix[:, :channels]) + ahead[...]).astype(BF16)
    grad[...] = (dot(table[...], matrix[:, channels:]) + mixed[...]).astype(BF16)


def final(seat, own, other, table, ahead, mixed, steps=2):
    atoms, channels = ahead.shape
    rows = atoms // steps
    block = pl.BlockSpec((rows, channels), lambda i: (i, 0))
    whole = pl.BlockSpec(own.shape, lambda i: (0, 0, 0), pipeline_mode=pl.Buffered(1))
    return pl.pallas_call(
        final_kernel,
        grid=(steps,),
        out_shape=(jax.ShapeDtypeStruct((atoms, channels), BF16),) * 2,
        in_specs=[
            SMEM,
            whole,
            whole,
            pl.BlockSpec((rows, table.shape[1]), lambda i: (i, 0)),
            block,
            block,
        ],
        out_specs=(block, block),
        scratch_shapes=[pltpu.VMEM((table.shape[1], 2 * channels), BF16)],
        compiler_params=pltpu.CompilerParams(vmem_limit_bytes=16 << 20),
        cost_estimate=pl.CostEstimate(flops=1 << 30, bytes_accessed=4 << 20, transcendentals=0),
        name="final",
    )(seat, own, other, table, in_hbm(ahead), in_hbm(mixed))


def body(
    embedding, cotangent, fractional, wave_index, tile_pairs, counts, wave_filter, short_weight
):
    devices = math.prod(lax.axis_size(name) for name in FINE)
    atoms_all = embedding.shape[0] * devices
    core, x, y = (lax.axis_index(name).astype(jnp.int32) for name in ("core", "x", "y"))
    seat = jnp.stack([core, core * 8 + (y & 1) * 4 + x])
    swap = [(0, 1), (1, 0)]

    listed = tile_pairs.T
    to_far = pack(seat[:1], embedding, cotangent, fractional, listed, counts)
    size = math.prod(lax.axis_size(name) for name in FINE)
    far = lax.ppermute(to_far, FINE, [(i, (i + (1 if i % 2 else -1)) % size) for i in range(size)])
    given = partial_sums(1 - seat[:1], wave_index, fractional, embedding, cotangent, True)
    given = lax.ppermute(given, "core", swap)
    kept = partial_sums(seat[:1], wave_index, fractional, embedding, cotangent, False)
    total = add(kept, given)
    chip = lax.all_to_all(total, ("y", "x"), 0, 0, tiled=True)
    to_close = pack(1 - seat[:1], embedding, cotangent, fractional, listed, counts)
    close = lax.ppermute(to_close, "core", swap)
    table = tables(wave_index, fractional)
    summed = plane_sum(chip)
    parts = lax.all_to_all(summed, ALONG_Z, 0, 0, tiled=True)
    tail = jnp.where(seat[0] == 0, far[PAIRS:ROWS, :TILE], close[PAIRS:ROWS, :TILE]).astype(jnp.int32)
    pairs_below, count_below = tail[0:2, : listed.shape[1]], tail[LIVE - PAIRS, 0:1]
    ahead, scale = near_ahead(
        seat, listed, counts, embedding, far, close, fractional, short_weight, wave_filter, atoms_all
    )
    mixed = near_behind(
        seat[:1], listed, counts, pairs_below, count_below, cotangent, far, close, fractional, short_weight
    )
    coeffs = lax.all_to_all(coefficients(parts, scale), ("y", "x"), 0, 0, tiled=True).reshape(256, 8, 128)
    other = lax.ppermute(coeffs, "core", swap)
    return final(seat, coeffs, other, table, ahead, mixed)


def solution(mesh):
    fine = Mesh(mesh.devices.reshape(4, 4, 4, 4, 2), FINE)
    rows, places, one = P(FINE, None), P(None, FINE), P(FINE)
    return jax.shard_map(
        body,
        mesh=fine,
        in_specs=(rows, rows, places, P(), rows, one, P(), P()),
        out_specs=(rows, rows),
        check_vma=False,
    )
```
